512 devices in a mesh: seq: 16 (over x_hi, z), head: 32 (over y, x_lo, core).
Axes of the slice: x: 4 (x_hi: 2, x_lo: 2; x = x_hi * 2 + x_lo), y: 8, z: 8, core: 2. Of those that a mesh axis runs over, the one named last changes fastest.
Arguments:
- query: bfloat16 [160, 2048, 128], P('head', 'seq'), may hold values from -1024 to 1024
- key: bfloat16 [160, 2048, 128], P('head', 'seq'), may hold values from -1024 to 1024
- value: bfloat16 [160, 2048, 128], P('head', 'seq'), may hold values from -6 to 6
- q_gain: float32 [40, 128], replicated, may hold values from 0.8 to 2
- k_gain: float32 [40, 128], replicated, may hold values from 0.8 to 2
- order: int32 [160, 2048], P('head', 'seq'), may hold values from 0 to 2047, as said below
- cluster_rows: int32 [160, 16], P('head'), may hold values from 0 to 256, as said below
- block_map: int32 [160, 32, 32], P('head'), may hold values 0 or 1
Outputs:
- attended: bfloat16 [160, 2048, 128], P('head', 'seq')
The draws below stay inside these ranges and needn't reach their ends.
Inputs may be any that keep to these rules, and one draw needn't show every extreme that they name: `order`: each stream's row lists every token row once: the rows of cluster 0 first, then those of cluster 1, and so on, in the counts of cluster_rows. `cluster_rows`: each stream's counts sum to 2048; of the 128 token rows of one seq index at most 16 belong to one cluster, and in every stream one cluster takes exactly 16 rows from every seq index.
All inputs are finite; a program needn't handle non-finite values. No bound on the sum of `block_map` on one device may be relied on, other than what follows from the above.
Results may differ from the reference program's by a relative error of at most 0.012.
The reference program's roundings to bfloat16 on the way count: a program that leaves them out, or rounds other values in their place, can miss the bound.
Values may be sent and summed in bfloat16 or wider, within the bound.
A program may use at most 64 MiB of HBM per device.

```python
import math
import jax
import jax.numpy as jnp
from jax import lax

H = 40
DH = 128
TOK_DEV = 128
BLOCK = 128
VIDEOS = 4
STREAMS = 160
LENGTH = 2048
CLUSTERS = 16
SLOT = 16
CAP = 256
NBALL = 32


def routing(key):
    base_key = jax.random.fold_in(key, 7001)
    key_heavy, key_pair, key_move, key_shuffle, key_rank = jax.random.split(base_key, 5)
    owners = CLUSTERS
    others = owners - 1
    heavy = jax.random.randint(key_heavy, (STREAMS,), 0, owners)
    rest_rows = TOK_DEV - SLOT
    other_slot = jnp.arange(others, dtype=jnp.int32)
    even_count = rest_rows // others + (other_slot < rest_rows % others).astype(jnp.int32)
    pair_noise = jax.random.randint(key_pair, (STREAMS, owners, others), 0, 2 ** 20) * others + other_slot
    pair_order = jnp.argsort(pair_noise, axis=-1).astype(jnp.int32)
    placed = even_count[pair_order]
    pair_count = others // 2
    if pair_count > 0:
        lead_count = placed[..., 0:2 * pair_count:2]
        follow_count = placed[..., 1:2 * pair_count:2]
        lowest = -jnp.minimum(follow_count, SLOT - lead_count)
        highest = jnp.minimum(lead_count, SLOT - follow_count)
        moved = jax.random.randint(key_move, lead_count.shape, lowest, highest + 1)
        paired = jnp.stack([lead_count - moved, follow_count + moved], axis=-1)
        paired = paired.reshape(STREAMS, owners, 2 * pair_count)
        placed = jnp.concatenate([paired, placed[..., 2 * pair_count:]], axis=-1)
    undo_order = jnp.argsort(pair_order, axis=-1)
    counts_other = jnp.take_along_axis(placed, undo_order, axis=-1)
    other_owner = other_slot[None, :] + (other_slot[None, :] >= heavy[:, None]).astype(jnp.int32)
    owner_axis = jnp.arange(owners, dtype=jnp.int32)
    spread_hit = (other_owner[:, :, None] == owner_axis).astype(jnp.int32)
    route_count = jnp.sum(counts_other[:, :, :, None] * spread_hit[:, None, :, :], axis=2)
    route_count = route_count + SLOT * (heavy[:, None, None] == owner_axis).astype(jnp.int32)
    route_bound = jnp.cumsum(route_count, axis=-1)
    token_slot = jnp.arange(TOK_DEV, dtype=jnp.int32)
    owner_label = jnp.sum((route_bound[:, :, None, :] <= token_slot[None, None, :, None]).astype(jnp.int32), axis=-1)
    shuffle_score = jax.random.randint(key_shuffle, (STREAMS, owners, TOK_DEV), 0, 2 ** 20) * TOK_DEV + token_slot
    owner_label = jnp.take_along_axis(owner_label, jnp.argsort(shuffle_score, axis=-1), axis=-1)
    owner_label = owner_label.reshape(STREAMS, LENGTH)
    token_ids = jnp.arange(LENGTH, dtype=jnp.int32)
    token_rank = jnp.argsort(jax.random.randint(key_rank, (STREAMS, LENGTH), 0, 2 ** 17) * LENGTH + token_ids, axis=-1)
    order_out = jnp.argsort(owner_label * LENGTH + token_rank.astype(jnp.int32), axis=-1).astype(jnp.int32)
    cluster_size = jnp.sum(route_count, axis=1).astype(jnp.int32)
    return (order_out, cluster_size)


def scaled(key, salt, rise_ratio):
    key_base, key_channel, key_token = jax.random.split(jax.random.fold_in(key, salt), 3)
    head_ids = (jnp.arange(STREAMS) % H).astype(jnp.float32)
    rise = rise_ratio ** (head_ids / (H - 1))
    channel_scale = jnp.exp(jax.random.uniform(key_channel, (STREAMS, 1, DH), minval=math.log(0.5), maxval=math.log(2.0)))
    token_scale = jnp.exp(jax.random.uniform(key_token, (VIDEOS, 1, LENGTH, 1), minval=0.0, maxval=math.log(10.0)))
    token_scale = jnp.broadcast_to(token_scale, (VIDEOS, H, LENGTH, 1)).reshape(STREAMS, LENGTH, 1)
    drawn = jax.random.normal(key_base, (STREAMS, LENGTH, DH), dtype=jnp.float32)
    return drawn * rise[:, None, None] * channel_scale * token_scale


def draw_order(key, part):
    return routing(key)[0]


def draw_cluster_rows(key, part):
    return routing(key)[1]


def draw_query(key, part):
    drawn = scaled(key, 7301, 1.94)
    return jnp.clip(drawn, -1024.0, 1024.0).astype(jnp.bfloat16)


def draw_key(key, part):
    drawn = scaled(key, 7302, 1.94)
    return jnp.clip(drawn, -1024.0, 1024.0).astype(jnp.bfloat16)


def touch_ends(result, rng, least, high):
    index_at = [jax.random.randint(jax.random.fold_in(rng, axis), (), 0, length) for axis, length in enumerate(result.shape)]
    longest = result.shape.index(max(result.shape))
    beside = index_at[:longest] + [(index_at[longest] + 1) % result.shape[longest]] + index_at[longest + 1:]
    return result.at[tuple(index_at)].set(least).at[tuple(beside)].set(high)


def block_scale(stream_key, dims, cuts, least, high):
    def one(dim, shards_of):
        draws = jax.random.uniform(jax.random.fold_in(jax.random.fold_in(stream_key, 6), dim), (shards_of,), jnp.float32, least / len(cuts), high / len(cuts))
        return jnp.repeat(jnp.exp(draws), dims[dim] // shards_of).reshape((-1,) + (1,) * (len(dims) - dim - 1))

    level = one(*cuts[0])
    for cut in cuts[1:]:
        level = level * one(*cut)
    return level


def bell_draw(key, shape, width, bound, cuts=(), kind=jnp.bfloat16):
    values = width * jax.random.normal(key, shape, jnp.float32)
    if cuts:
        values = values * block_scale(key, shape, cuts, -0.22, 0.18)
    return jnp.clip(values, -bound, bound).astype(kind)


def setup_inputs(seed: int = 0) -> dict:
    splits = jax.random.split(jax.random.key(seed), 9)
    query = draw_query(jax.random.fold_in(splits[8], 71), 0)
    key = draw_key(jax.random.fold_in(splits[8], 71), 0)
    value = bell_draw(splits[2], (STREAMS, LENGTH, DH), 1.0, 6.0, ((0, 32), (1, 16)))
    q_gain = jnp.clip(jnp.exp(jax.random.uniform(splits[3], (H, DH), jnp.float32, math.log(0.8), math.log(2.0))), 0.8, 2.0)
    k_gain = jnp.clip(jnp.exp(jax.random.uniform(splits[4], (H, DH), jnp.float32, math.log(0.8), math.log(2.0))), 0.8, 2.0)
    order = draw_order(jax.random.fold_in(splits[8], 71), 0)
    cluster_rows = draw_cluster_rows(jax.random.fold_in(splits[8], 71), 0)
    block_map = touch_ends((jax.random.randint(splits[7], (STREAMS, NBALL, NBALL), 0, 2) < 1).astype(jnp.int32), jax.random.fold_in(splits[7], 1), 0, 1)
    return {"query": query, "key": key, "value": value, "q_gain": q_gain, "k_gain": k_gain, "order": order, "cluster_rows": cluster_rows, "block_map": block_map}


epsilon = 1e-06

def reference(query, key, value, q_gain, k_gain, order, cluster_rows, block_map):
    streams, seq_length, head_width = query.shape
    head_count = q_gain.shape[0]
    videos = streams // head_count

    def normalize(rows, gain):
        widened = rows.astype(jnp.float32).reshape(videos, head_count, seq_length, head_width)
        mean_square = lax.optimization_barrier(jnp.mean(jnp.square(widened), axis=(1, 3), keepdims=True))
        normed = widened * lax.rsqrt(mean_square + epsilon) * gain[None, :, None, :]
        return normed.reshape(streams, seq_length, head_width).astype(jnp.bfloat16)
    normed_q = normalize(query, q_gain)
    normed_k = normalize(key, k_gain)
    blocks_per = CAP // BLOCK
    score_scale = head_width ** (-0.5)

    def one_stream(inputs):
        stream_q, stream_k, stream_v, stream_order, stream_rows, stream_map = inputs
        positions = jnp.arange(seq_length, dtype=jnp.int32)
        inverse = jnp.zeros((seq_length,), jnp.int32).at[stream_order].set(positions)
        starts = jnp.cumsum(stream_rows, dtype=jnp.int32) - stream_rows
        owner_id = lax.optimization_barrier(jnp.sum((starts[None, :] <= inverse[:, None]).astype(jnp.int32), axis=1, dtype=jnp.int32)) - 1
        within_row = inverse - starts[owner_id]
        block_id = owner_id * blocks_per + within_row // BLOCK
        allowed = (stream_map[block_id][:, block_id] == 1) | (block_id[:, None] == block_id[None, :])
        scores = jnp.dot(stream_q, stream_k.T, preferred_element_type=jnp.float32) * score_scale
        masked = jnp.where(allowed, scores, -jnp.inf)
        row_peak = lax.optimization_barrier(jnp.max(masked, axis=1, keepdims=True))
        probs = jnp.where(allowed, jnp.exp(masked - row_peak), 0.0)
        denom_sum = lax.optimization_barrier(jnp.sum(probs, axis=1, keepdims=True))
        mixed = jnp.dot(probs.astype(jnp.bfloat16), stream_v, preferred_element_type=jnp.float32) / denom_sum
        return mixed.astype(jnp.bfloat16)
    return lax.map(one_stream, (normed_q, normed_k, value, order, cluster_rows, block_map))
```

```python
import math

import jax
import jax.numpy as jnp
from jax import lax
from jax.experimental import pallas as pl
from jax.experimental.pallas import tpu as pltpu
from jax.sharding import PartitionSpec as P

MESH = pl.DeviceIdType.MESH
F32 = jnp.float32
BF16 = jnp.bfloat16

EPS = 1e-06
ROWS = 128
Z = 8
STREAMS = 5
HEADS = 40
GROUP = 8
CLUSTERS = 16
BLOCKS = 32
MASKED = -(2.0**30)
NEAR_FIRST = (0, 1, 7, 2, 6, 3, 5, 4)
FAR_FIRST = (4, 3, 5, 2, 6, 1, 7, 0)
KEY_CHUNK = 512


def owner_of(z, shift, core):
    v = lax.rem(z - shift + 3 * core + 16, Z)
    stream = jnp.minimum(v - 3 * core * (v // 7), STREAMS - 1)
    busy = jnp.logical_or(v < STREAMS - core, core * v == 7)
    return stream, busy


def kernel(
    q_hbm, k_hbm, v_hbm, qg_ref, kg_ref, order_ref, rows_ref, map_ref, out_ref,
    qraw, kraw, qn, kn, sum_out, sum_in, ord_out, ord_in, kbuf, vbuf, qbuf, obuf,
    oht, mbuf, s_scr, bt_scr, a_scr,
    raw_sem, sum_send, sum_recv, ord_send, ord_recv, kv_send, kv_recv, fwd_send, fwd_recv,
    ofw_send, ofw_recv, out_send, out_recv,
):
    me = lax.axis_index("seq")
    head = lax.axis_index("head")
    half, z = me // Z, lax.rem(me, Z)
    shift = 2 * lax.rem(head // 2, 2)
    core = lax.rem(head, 2)
    member = lax.rem(head, GROUP)
    video = head - member
    mine, busy = owner_of(z, shift, core)
    partner = {"seq": (1 - half) * Z + z}

    def column(d):
        return lax.rem(z + d, Z)

    barrier = pltpu.get_barrier_semaphore()
    for d in range(1, Z):
        pl.semaphore_signal(
            barrier, inc=1, device_id={"seq": half * Z + column(d)}, device_id_type=MESH
        )
        pl.semaphore_signal(
            barrier,
            inc=1,
            device_id={"head": video + lax.rem(member + d, GROUP)},
            device_id_type=MESH,
        )
    pl.semaphore_signal(barrier, inc=1, device_id=partner, device_id_type=MESH)

    q_in = pltpu.make_async_copy(q_hbm, qraw, raw_sem.at[0])
    k_in = pltpu.make_async_copy(k_hbm, kraw, raw_sem.at[1])
    q_in.start()
    k_in.start()
    sum_out[...] = jnp.zeros((8, ROWS), F32)
    for j in range(STREAMS):
        ord_out[j] = jnp.broadcast_to(order_ref[pl.ds(j, 1), :], (8, ROWS))

    def squares(raw):
        total = jnp.zeros((ROWS, ROWS), F32)
        for j in range(STREAMS):
            x = raw[j].astype(F32)
            total = total + x * x
        return jnp.sum(total.T, axis=0, keepdims=True)

    q_in.wait()
    sum_out[pl.ds(0, 1), :] = squares(qraw)
    k_in.wait()
    sum_out[pl.ds(1, 1), :] = squares(kraw)

    pl.semaphore_wait(barrier, 2 * (Z - 1) + 1)

    def sum_copy(d):
        return pltpu.make_async_remote_copy(
            src_ref=sum_out,
            dst_ref=sum_in.at[member],
            send_sem=sum_send.at[d - 1],
            recv_sem=sum_recv.at[member],
            device_id={"head": video + lax.rem(member + d, GROUP)},
            device_id_type=MESH,
        )

    def sum_arrival(d):
        slot = lax.rem(member + d, GROUP)
        return pltpu.make_async_remote_copy(
            src_ref=sum_out,
            dst_ref=sum_in.at[slot],
            send_sem=sum_send.at[d - 1],
            recv_sem=sum_recv.at[slot],
            device_id={"head": video + slot},
            device_id_type=MESH,
        )

    for d in range(1, GROUP):
        sum_copy(d).start()

    def piece(kind, d):
        to = column(d)
        stream, _ = owner_of(to, shift, core)
        src = (v_hbm, kn, qn)[kind].at[stream]
        dst = (vbuf.at[me], kbuf.at[me], qbuf.at[z])[kind]
        return pltpu.make_async_remote_copy(
            src_ref=src,
            dst_ref=dst,
            send_sem=kv_send.at[kind, d],
            recv_sem=kv_recv.at[kind, z],
            device_id={"seq": half * Z + to},
            device_id_type=MESH,
        )

    def own_piece(kind):
        src = (v_hbm, kn, qn)[kind].at[mine]
        dst = (vbuf.at[me], kbuf.at[me], qbuf.at[z])[kind]
        return pltpu.make_async_copy(src, dst, kv_recv.at[kind, z])

    def arrival(kind, d):
        slot = column(d)
        dst = (vbuf.at[half * Z + slot], kbuf.at[half * Z + slot], qbuf.at[slot])[kind]
        return pltpu.make_async_remote_copy(
            src_ref=dst,
            dst_ref=dst,
            send_sem=kv_send.at[kind, d],
            recv_sem=kv_recv.at[kind, slot],
            device_id={"seq": half * Z + slot},
            device_id_type=MESH,
        )

    def order_piece(d):
        to = column(d)
        stream, _ = owner_of(to, shift, core)
        return pltpu.make_async_remote_copy(
            src_ref=ord_out.at[stream],
            dst_ref=ord_in.at[half, z],
            send_sem=ord_send.at[d],
            recv_sem=ord_recv.at[z],
            device_id={"seq": half * Z + to},
            device_id_type=MESH,
        )

    def own_order():
        return pltpu.make_async_copy(ord_out.at[mine], ord_in.at[half, z], ord_recv.at[z])

    def order_arrival(d):
        slot = column(d)
        return pltpu.make_async_remote_copy(
            src_ref=ord_in.at[half, slot],
            dst_ref=ord_in.at[half, slot],
            send_sem=ord_send.at[d],
            recv_sem=ord_recv.at[slot],
            device_id={"seq": half * Z + slot},
            device_id_type=MESH,
        )

    def forward(kind, slot, side):
        buf = (vbuf, kbuf)[kind]
        return pltpu.make_async_remote_copy(
            src_ref=buf.at[side * Z + slot],
            dst_ref=buf.at[side * Z + slot],
            send_sem=fwd_send.at[kind, slot],
            recv_sem=fwd_recv.at[kind, slot],
            device_id=partner,
            device_id_type=MESH,
        )

    def order_forward(side):
        return pltpu.make_async_remote_copy(
            src_ref=ord_in.at[side],
            dst_ref=ord_in.at[side],
            send_sem=ofw_send.at[0],
            recv_sem=ofw_recv.at[0],
            device_id=partner,
            device_id_type=MESH,
        )

    def to_all(make):
        for d in FAR_FIRST[:-1]:
            _, there = owner_of(column(d), shift, core)

            @pl.when(there)
            def _(d=d):
                make(d)

    to_all(lambda d: order_piece(d).start())
    to_all(lambda d: piece(0, d).start())

    @pl.when(busy)
    def _():
        own_order().start()
        own_piece(0).start()

    total = sum_out[...]
    for d in range(1, GROUP):
        sum_arrival(d).wait_recv()
    for d in range(1, GROUP):
        total = total + sum_in[lax.rem(member + d, GROUP)]
    scale = lax.rsqrt(total * (1.0 / (HEADS * ROWS)) + EPS)

    def normalize(raw, gains, row, out):
        by_row = jnp.broadcast_to(scale[row : row + 1, :], (ROWS, ROWS)).T
        for j in range(STREAMS):
            gain = gains[pl.ds(member * STREAMS + j, 1), :]
            out[j] = (raw[j].astype(F32) * by_row * gain).astype(BF16)

    normalize(kraw, kg_ref, 1, kn)
    normalize(qraw, qg_ref, 0, qn)
    to_all(lambda d: piece(1, d).start())
    to_all(lambda d: piece(2, d).start())

    def result(slot):
        return pltpu.make_async_remote_copy(
            src_ref=obuf.at[slot],
            dst_ref=out_ref.at[mine],
            send_sem=out_send.at[slot],
            recv_sem=out_recv.at[mine],
            device_id={"seq": half * Z + slot},
            device_id_type=MESH,
        )

    def own_result():
        return pltpu.make_async_copy(obuf.at[z], out_ref.at[mine], out_recv.at[mine])

    def result_arrival(d):
        stream, _ = owner_of(column(d), shift, core)
        return pltpu.make_async_remote_copy(
            src_ref=obuf.at[0],
            dst_ref=out_ref.at[stream],
            send_sem=out_send.at[0],
            recv_sem=out_recv.at[stream],
            device_id={"seq": half * Z + column(d)},
            device_id_type=MESH,
        )

    @pl.when(busy)
    def _():
        own_piece(1).start()
        own_piece(2).start()
        own_order().wait()
        for d in NEAR_FIRST[1:]:
            order_arrival(d).wait_recv()
        order_forward(half).start()
        own_piece(0).wait()
        forward(0, z, half).start()
        for d in NEAR_FIRST[1:]:
            arrival(0, d).wait_recv()
            forward(0, column(d), half).start()
        own_piece(1).wait()
        forward(1, z, half).start()
        for d in NEAR_FIRST[1:]:
            arrival(1, d).wait_recv()
            forward(1, column(d), half).start()

        order_forward(1 - half).wait_recv()
        tokens = ord_in[:, :, 0, :].reshape(CLUSTERS, ROWS)
        place = lax.broadcasted_iota(jnp.int32, (CLUSTERS, ROWS), 0) * ROWS
        place = place + lax.broadcasted_iota(jnp.int32, (CLUSTERS, ROWS), 1)
        owner = jnp.full((CLUSTERS, ROWS), -1, jnp.int32)
        start = jnp.zeros((CLUSTERS, ROWS), jnp.int32)
        at = jnp.int32(0)
        for o in range(CLUSTERS):
            begun = place >= at
            owner = owner + begun.astype(jnp.int32)
            start = jnp.where(begun, at, start)
            at = at + rows_ref[mine, o]
        block = (owner * 2 + jnp.right_shift(place - start, 7)).astype(F32)
        high = jnp.right_shift(tokens, 7)
        low = jnp.bitwise_and(tokens, ROWS - 1)
        digit = lax.broadcasted_iota(jnp.int32, (ROWS, ROWS), 0)
        digit_high = lax.broadcasted_iota(jnp.int32, (CLUSTERS, ROWS), 0)
        for i in range(CLUSTERS):
            span = pl.ds(i * ROWS, ROWS)
            hit = digit == jnp.broadcast_to(low[i : i + 1], (ROWS, ROWS))
            bt_scr[:, span] = jnp.where(hit, 1.0, 0.0).astype(BF16)
            hit = digit_high == jnp.broadcast_to(high[i : i + 1], (CLUSTERS, ROWS))
            here = jnp.broadcast_to(block[i : i + 1], (CLUSTERS, ROWS))
            a_scr[:, span] = jnp.where(hit, here, 0.0).astype(BF16)
        by_low = lax.dot_general(
            bt_scr[...], a_scr[...], (((1,), (1,)), ((), ())), preferred_element_type=F32
        ).astype(BF16)
        lane = lax.broadcasted_iota(jnp.int32, (CLUSTERS, ROWS * CLUSTERS), 1)
        spread = jnp.right_shift(lane, 7) == lax.broadcasted_iota(
            jnp.int32, (CLUSTERS, ROWS * CLUSTERS), 0
        )
        wide = jnp.dot(
            by_low, jnp.where(spread, 1.0, 0.0).astype(BF16), preferred_element_type=F32
        )
        which = lax.broadcasted_iota(jnp.int32, (ROWS, ROWS), 1).astype(F32)
        for i in range(CLUSTERS):
            hit = wide[:, i * ROWS : (i + 1) * ROWS] == which
            oht[i] = jnp.where(hit, 1.0, 0.0).astype(BF16)
        mbuf[...] = jnp.zeros((ROWS, ROWS), BF16)
        same = lax.broadcasted_iota(jnp.int32, (BLOCKS, BLOCKS), 0) == (
            lax.broadcasted_iota(jnp.int32, (BLOCKS, BLOCKS), 1)
        )
        open_ = jnp.logical_or(map_ref[mine] == 1, same)
        mbuf[pl.ds(0, BLOCKS), pl.ds(0, BLOCKS)] = jnp.where(open_, 0.0, MASKED).astype(BF16)

        own_piece(2).wait()
        for d in NEAR_FIRST[1:]:
            arrival(2, d).wait_recv()
        for kind in range(2):
            for d in NEAR_FIRST:
                forward(kind, column(d), 1 - half).wait_recv()

        factor = math.log2(math.e) / math.sqrt(ROWS)
        chunks = CLUSTERS * ROWS // KEY_CHUNK
        per = KEY_CHUNK // ROWS

        def unit(t, carry):
            d = 4 + (1 - 2 * lax.rem(t, 2)) * ((t + 1) // 2)
            slot = column(d)
            bias = jnp.dot(oht[half * Z + slot], mbuf[...], preferred_element_type=F32)
            left = jnp.concatenate([qbuf[slot], bias.astype(BF16)], axis=1)
            peak = jnp.full((ROWS, 1), -jnp.inf, F32)
            for i in range(chunks):
                keys = kbuf[pl.ds(i * per, per)].reshape(KEY_CHUNK, ROWS)
                tags = oht[pl.ds(i * per, per)].reshape(KEY_CHUNK, ROWS)
                scores = lax.dot_general(
                    left,
                    jnp.concatenate([keys, tags], axis=1),
                    (((1,), (1,)), ((), ())),
                    preferred_element_type=F32,
                )
                s_scr[:, pl.ds(i * KEY_CHUNK, KEY_CHUNK)] = scores
                peak = jnp.maximum(peak, jnp.max(scores, axis=1, keepdims=True))
            denom = jnp.zeros((ROWS, 1), F32)
            mixed = jnp.zeros((ROWS, ROWS), F32)
            for i in range(chunks):
                p = jnp.exp2((s_scr[:, pl.ds(i * KEY_CHUNK, KEY_CHUNK)] - peak) * factor)
                denom = denom + jnp.sum(p, axis=1, keepdims=True)
                values = vbuf[pl.ds(i * per, per)].reshape(KEY_CHUNK, ROWS)
                mixed = mixed + jnp.dot(p.astype(BF16), values, preferred_element_type=F32)
            obuf[slot] = (mixed / denom).astype(BF16)

            @pl.when(t < Z - 1)
            def _():
                result(slot).start()

            return carry

        lax.fori_loop(0, Z, unit, 0)
        own_result().start()

    for d in range(1, GROUP):
        sum_copy(d).wait_send()
    to_all(lambda d: order_piece(d).wait_send())
    for kind in range(3):
        to_all(lambda d, kind=kind: piece(kind, d).wait_send())

    @pl.when(busy)
    def _():
        order_forward(half).wait_send()
        for kind in range(2):
            for d in NEAR_FIRST:
                forward(kind, column(d), half).wait_send()
        for d in FAR_FIRST[:-1]:
            result(column(d)).wait_send()
        own_result().wait()

    to_all(lambda d: result_arrival(d).wait_recv())


def local(query, key, value, q_gain, k_gain, order, cluster_rows, block_map):
    streams = query.shape[0]
    any_ = pl.BlockSpec(memory_space=pl.ANY)
    vmem = pl.BlockSpec(memory_space=pltpu.VMEM)
    smem = pl.BlockSpec(memory_space=pltpu.SMEM)
    sems = pltpu.SemaphoreType.DMA
    return pl.pallas_call(
        kernel,
        out_shape=jax.ShapeDtypeStruct((streams, ROWS, ROWS), BF16),
        in_specs=[any_, any_, any_, vmem, vmem, vmem, smem, vmem],
        out_specs=any_,
        scratch_shapes=[
            pltpu.VMEM((STREAMS, ROWS, ROWS), BF16),
            pltpu.VMEM((STREAMS, ROWS, ROWS), BF16),
            pltpu.VMEM((STREAMS, ROWS, ROWS), BF16),
            pltpu.VMEM((STREAMS, ROWS, ROWS), BF16),
            pltpu.VMEM((8, ROWS), F32),
            pltpu.VMEM((GROUP, 8, ROWS), F32),
            pltpu.VMEM((STREAMS, 8, ROWS), jnp.int32),
            pltpu.VMEM((2, Z, 8, ROWS), jnp.int32),
            pltpu.VMEM((2 * Z, ROWS, ROWS), BF16),
            pltpu.VMEM((2 * Z, ROWS, ROWS), BF16),
            pltpu.VMEM((Z, ROWS, ROWS), BF16),
            pltpu.VMEM((Z, ROWS, ROWS), BF16),
            pltpu.VMEM((2 * Z, ROWS, ROWS), BF16),
            pltpu.VMEM((ROWS, ROWS), BF16),
            pltpu.VMEM((ROWS, 2 * Z * ROWS), F32),
            pltpu.VMEM((ROWS, 2 * Z * ROWS), BF16),
            pltpu.VMEM((CLUSTERS, 2 * Z * ROWS), BF16),
            sems((2,)),
            sems((GROUP - 1,)),
            sems((GROUP,)),
            sems((Z,)),
            sems((Z,)),
            sems((3, Z)),
            sems((3, Z)),
            sems((2, Z)),
            sems((2, Z)),
            sems((1,)),
            sems((1,)),
            sems((Z,)),
            sems((STREAMS,)),
        ],
        compiler_params=pltpu.CompilerParams(collective_id=0, has_side_effects=True),
        name="attend",
    )(query, key, value, q_gain, k_gain, order, cluster_rows, block_map)


def solution(mesh):
    return jax.shard_map(
        local,
        mesh=mesh,
        in_specs=(
            P("head", "seq", None),
            P("head", "seq", None),
            P("head", "seq", None),
            P(),
            P(),
            P("head", "seq"),
            P("head", None),
            P("head", None, None),
        ),
        out_specs=P("head", "seq", None),
        check_vma=False,
    )
```

```python
import math

import jax
import jax.numpy as jnp
from jax import lax
from jax.experimental import pallas as pl
from jax.experimental.pallas import tpu as pltpu
from jax.sharding import PartitionSpec as P

MESH = pl.DeviceIdType.MESH
F32 = jnp.float32
BF16 = jnp.bfloat16

EPS = 1e-06
ROWS = 128
Z = 8
STREAMS = 5
HEADS = 40
GROUP = 8
CLUSTERS = 16
BLOCKS = 32
MASKED = -(2.0**30)
FAR_FIRST = (4, 3, 5, 2, 6, 1, 7, 0)
KEY_CHUNK = 512
PER = KEY_CHUNK // ROWS
PARTS = Z // PER


def owner_of(z, shift, core):
    v = lax.rem(z - shift + 3 * core + 16, Z)
    stream = jnp.minimum(v - 3 * core * (v // 7), STREAMS - 1)
    busy = jnp.logical_or(v < STREAMS - core, core * v == 7)
    return stream, busy


def kernel(
    q_hbm, k_hbm, v_hbm, qg_hbm, kg_hbm, order_hbm, rows_hbm, map_hbm, out_ref,
    qg_ref, kg_ref, order_ref, rows_ref, map_ref, qraw, kraw, qn, kn, sum_out, sum_in, ord_out, ord_in, kbuf, vbuf, qbuf, obuf,
    oht, mbuf, lbuf, peaks, denoms, mixes, s_scr, bt_scr, a_scr,
    raw_sem, sum_send, sum_recv, ord_send, ord_recv, kv_send, kv_recv, fwd_send, fwd_recv,
    ofw_send, ofw_recv, out_send, out_recv,
):
    me = lax.axis_index("seq")
    head = lax.axis_index("head")
    half, z = me // Z, lax.rem(me, Z)
    shift = 2 * lax.rem(head // 2, 2)
    core = lax.rem(head, 2)
    member = lax.rem(head, GROUP)
    video = head - member
    mine, busy = owner_of(z, shift, core)
    partner = {"seq": (1 - half) * Z + z}

    def column(d):
        return lax.rem(z + d, Z)

    barrier = pltpu.get_barrier_semaphore()
    for d in range(1, Z):
        pl.semaphore_signal(
            barrier, inc=1, device_id={"seq": half * Z + column(d)}, device_id_type=MESH
        )
        pl.semaphore_signal(
            barrier,
            inc=1,
            device_id={"head": video + lax.rem(member + d, GROUP)},
            device_id_type=MESH,
        )
    pl.semaphore_signal(barrier, inc=1, device_id=partner, device_id_type=MESH)

    q_in = pltpu.make_async_copy(q_hbm, qraw, raw_sem.at[0])
    k_in = pltpu.make_async_copy(k_hbm, kraw, raw_sem.at[1])
    small = [
        pltpu.make_async_copy(src, dst, raw_sem.at[2 + i])
        for i, (src, dst) in enumerate(
            (
                (order_hbm, order_ref),
                (kg_hbm, kg_ref),
                (qg_hbm, qg_ref),
                (rows_hbm, rows_ref),
                (map_hbm, map_ref),
            )
        )
    ]
    small[0].start()
    q_in.start()
    k_in.start()
    for copy in small[1:]:
        copy.start()
    pl.semaphore_wait(barrier, 2 * (Z - 1) + 1)

    def sum_copy(d):
        return pltpu.make_async_remote_copy(
            src_ref=sum_out,
            dst_ref=sum_in.at[member],
            send_sem=sum_send.at[d - 1],
            recv_sem=sum_recv.at[member],
            device_id={"head": video + lax.rem(member + d, GROUP)},
            device_id_type=MESH,
        )

    def sum_arrival(d):
        slot = lax.rem(member + d, GROUP)
        return pltpu.make_async_remote_copy(
            src_ref=sum_out,
            dst_ref=sum_in.at[slot],
            send_sem=sum_send.at[d - 1],
            recv_sem=sum_recv.at[slot],
            device_id={"head": video + slot},
            device_id_type=MESH,
        )

    def piece(kind, d):
        to = column(d)
        stream, _ = owner_of(to, shift, core)
        src = (v_hbm, kn, qn)[kind].at[stream]
        dst = (vbuf.at[me], kbuf.at[me], qbuf.at[z])[kind]
        return pltpu.make_async_remote_copy(
            src_ref=src,
            dst_ref=dst,
            send_sem=kv_send.at[kind, d],
            recv_sem=kv_recv.at[kind, z],
            device_id={"seq": half * Z + to},
            device_id_type=MESH,
        )

    def own_piece(kind):
        src = (v_hbm, kn, qn)[kind].at[mine]
        dst = (vbuf.at[me], kbuf.at[me], qbuf.at[z])[kind]
        return pltpu.make_async_copy(src, dst, kv_recv.at[kind, z])

    def arrival(kind, d):
        slot = column(d)
        dst = (vbuf.at[half * Z + slot], kbuf.at[half * Z + slot], qbuf.at[slot])[kind]
        return pltpu.make_async_remote_copy(
            src_ref=dst,
            dst_ref=dst,
            send_sem=kv_send.at[kind, d],
            recv_sem=kv_recv.at[kind, slot],
            device_id={"seq": half * Z + slot},
            device_id_type=MESH,
        )

    def order_piece(d):
        to = column(d)
        stream, _ = owner_of(to, shift, core)
        return pltpu.make_async_remote_copy(
            src_ref=ord_out.at[stream],
            dst_ref=ord_in.at[half, z],
            send_sem=ord_send.at[d],
            recv_sem=ord_recv.at[z],
            device_id={"seq": half * Z + to},
            device_id_type=MESH,
        )

    def own_order():
        return pltpu.make_async_copy(ord_out.at[mine], ord_in.at[half, z], ord_recv.at[z])

    def order_arrival(d):
        slot = column(d)
        return pltpu.make_async_remote_copy(
            src_ref=ord_in.at[half, slot],
            dst_ref=ord_in.at[half, slot],
            send_sem=ord_send.at[d],
            recv_sem=ord_recv.at[slot],
            device_id={"seq": half * Z + slot},
            device_id_type=MESH,
        )

    def forward(kind, slot, side):
        buf = (vbuf, kbuf)[kind]
        return pltpu.make_async_remote_copy(
            src_ref=buf.at[side * Z + slot],
            dst_ref=buf.at[side * Z + slot],
            send_sem=fwd_send.at[kind, slot],
            recv_sem=fwd_recv.at[kind, slot],
            device_id=partner,
            device_id_type=MESH,
        )

    def order_forward(side):
        return pltpu.make_async_remote_copy(
            src_ref=ord_in.at[side],
            dst_ref=ord_in.at[side],
            send_sem=ofw_send.at[0],
            recv_sem=ofw_recv.at[0],
            device_id=partner,
            device_id_type=MESH,
        )

    def to_all(make):
        for d in FAR_FIRST[:-1]:
            _, there = owner_of(column(d), shift, core)

            @pl.when(there)
            def _(d=d):
                make(d)

    to_all(lambda d: piece(0, d).start())
    small[0].wait()
    sum_out[...] = jnp.zeros((8, ROWS), F32)
    for j in range(STREAMS):
        ord_out[j] = jnp.broadcast_to(order_ref[pl.ds(j, 1), :], (8, ROWS))

    def squares(raw):
        total = jnp.zeros((ROWS, ROWS), F32)
        for j in range(STREAMS):
            x = raw[j].astype(F32)
            total = total + x * x
        return jnp.sum(total.T, axis=0, keepdims=True)
    to_all(lambda d: order_piece(d).start())

    @pl.when(busy)
    def _():
        own_order().start()
        own_piece(0).start()

    q_in.wait()
    sum_out[pl.ds(0, 1), :] = squares(qraw)
    k_in.wait()
    sum_out[pl.ds(1, 1), :] = squares(kraw)
    for d in range(1, GROUP):
        sum_copy(d).start()
    for copy in small[1:]:
        copy.wait()
    total = sum_out[...]
    for d in range(1, GROUP):
        sum_arrival(d).wait_recv()
    for d in range(1, GROUP):
        total = total + sum_in[lax.rem(member + d, GROUP)]
    scale = lax.rsqrt(total * (1.0 / (HEADS * ROWS)) + EPS)

    def by_row(row):
        return jnp.broadcast_to(scale[row : row + 1, :], (ROWS, ROWS)).T

    def normalize(kind, d, rows):
        stream, _ = owner_of(column(d), shift, core)
        raw, gains, out = ((kraw, kg_ref, kn), (qraw, qg_ref, qn))[kind - 1]
        gain = gains[pl.ds(member * STREAMS + stream, 1), :]
        out[stream] = (raw[stream].astype(F32) * rows * gain).astype(BF16)

    for kind in (1, 2):
        rows = by_row(2 - kind)

        def ready(d, kind=kind, rows=rows):
            normalize(kind, d, rows)
            piece(kind, d).start()

        to_all(ready)

        @pl.when(busy)
        def _(kind=kind, rows=rows):
            normalize(kind, 0, rows)
            own_piece(kind).start()

    def result(slot):
        return pltpu.make_async_remote_copy(
            src_ref=obuf.at[slot],
            dst_ref=out_ref.at[mine],
            send_sem=out_send.at[slot],
            recv_sem=out_recv.at[mine],
            device_id={"seq": half * Z + slot},
            device_id_type=MESH,
        )

    def own_result():
        return pltpu.make_async_copy(obuf.at[z], out_ref.at[mine], out_recv.at[mine])

    def result_arrival(d):
        stream, _ = owner_of(column(d), shift, core)
        return pltpu.make_async_remote_copy(
            src_ref=obuf.at[0],
            dst_ref=out_ref.at[stream],
            send_sem=out_send.at[0],
            recv_sem=out_recv.at[stream],
            device_id={"seq": half * Z + column(d)},
            device_id_type=MESH,
        )

    @pl.when(busy)
    def _():
        own_piece(0).wait()
        forward(0, z, half).start()
        for d in FAR_FIRST[:-1]:
            arrival(0, d).wait_recv()
            forward(0, column(d), half).start()
        own_order().wait()
        for d in FAR_FIRST[:-1]:
            order_arrival(d).wait_recv()
        order_forward(half).start()
        own_piece(1).wait()
        forward(1, z, half).start()
        for d in FAR_FIRST[:-1]:
            arrival(1, d).wait_recv()
            forward(1, column(d), half).start()

        order_forward(1 - half).wait_recv()
        tokens = ord_in[:, :, 0, :].reshape(CLUSTERS, ROWS)
        place = lax.broadcasted_iota(jnp.int32, (CLUSTERS, ROWS), 0) * ROWS
        place = place + lax.broadcasted_iota(jnp.int32, (CLUSTERS, ROWS), 1)
        owner = jnp.full((CLUSTERS, ROWS), -1, jnp.int32)
        start = jnp.zeros((CLUSTERS, ROWS), jnp.int32)
        at = jnp.int32(0)
        for o in range(CLUSTERS):
            begun = place >= at
            owner = owner + begun.astype(jnp.int32)
            start = jnp.where(begun, at, start)
            at = at + rows_ref[mine, o]
        block = (owner * 2 + jnp.right_shift(place - start, 7)).astype(F32)
        high = jnp.right_shift(tokens, 7)
        low = jnp.bitwise_and(tokens, ROWS - 1)
        digit = lax.broadcasted_iota(jnp.int32, (ROWS, ROWS), 0)
        digit_high = lax.broadcasted_iota(jnp.int32, (CLUSTERS, ROWS), 0)
        for i in range(CLUSTERS):
            span = pl.ds(i * ROWS, ROWS)
            hit = digit == jnp.broadcast_to(low[i : i + 1], (ROWS, ROWS))
            bt_scr[:, span] = jnp.where(hit, 1.0, 0.0).astype(BF16)
            hit = digit_high == jnp.broadcast_to(high[i : i + 1], (CLUSTERS, ROWS))
            here = jnp.broadcast_to(block[i : i + 1], (CLUSTERS, ROWS))
            a_scr[:, span] = jnp.where(hit, here, 0.0).astype(BF16)
        by_low = lax.dot_general(
            bt_scr[...], a_scr[...], (((1,), (1,)), ((), ())), preferred_element_type=F32
        ).astype(BF16)
        lane = lax.broadcasted_iota(jnp.int32, (CLUSTERS, ROWS * CLUSTERS), 1)
        spread = jnp.right_shift(lane, 7) == lax.broadcasted_iota(
            jnp.int32, (CLUSTERS, ROWS * CLUSTERS), 0
        )
        wide = jnp.dot(
            by_low, jnp.where(spread, 1.0, 0.0).astype(BF16), preferred_element_type=F32
        )
        which = lax.broadcasted_iota(jnp.int32, (ROWS, ROWS), 1).astype(F32)
        for i in range(CLUSTERS):
            hit = wide[:, i * ROWS : (i + 1) * ROWS] == which
            oht[i] = jnp.where(hit, 1.0, 0.0).astype(BF16)
        mbuf[...] = jnp.zeros((ROWS, ROWS), BF16)
        same = lax.broadcasted_iota(jnp.int32, (BLOCKS, BLOCKS), 0) == (
            lax.broadcasted_iota(jnp.int32, (BLOCKS, BLOCKS), 1)
        )
        open_ = jnp.logical_or(map_ref[mine] == 1, same)
        mbuf[pl.ds(0, BLOCKS), pl.ds(0, BLOCKS)] = jnp.where(open_, 0.0, MASKED).astype(BF16)

        factor = math.log2(math.e) / math.sqrt(ROWS)

        def weigh(left, side, start):
            peak = start
            for i in range(PARTS):
                span = pl.ds(side * Z + i * PER, PER)
                scores = lax.dot_general(
                    left,
                    jnp.concatenate(
                        [
                            kbuf[span].reshape(KEY_CHUNK, ROWS),
                            oht[span].reshape(KEY_CHUNK, ROWS),
                        ],
                        axis=1,
                    ),
                    (((1,), (1,)), ((), ())),
                    preferred_element_type=F32,
                )
                s_scr[:, pl.ds(i * KEY_CHUNK, KEY_CHUNK)] = scores
                peak = jnp.maximum(peak, jnp.max(scores, axis=1, keepdims=True))
            denom = jnp.zeros((2 * ROWS, 1), F32)
            mixed = jnp.zeros((2 * ROWS, ROWS), F32)
            for i in range(PARTS):
                span = pl.ds(side * Z + i * PER, PER)
                p = jnp.exp2((s_scr[:, pl.ds(i * KEY_CHUNK, KEY_CHUNK)] - peak) * factor)
                denom = denom + jnp.sum(p, axis=1, keepdims=True)
                values = vbuf[span].reshape(KEY_CHUNK, ROWS)
                mixed = mixed + jnp.dot(p.astype(BF16), values, preferred_element_type=F32)
            return peak, denom, mixed

        def near_half(t, carry):
            first, second = lax.rem(4 - t, 4), 4 + t

            @pl.when(t == 0)
            def _():
                own_piece(2).wait()

            @pl.when(t > 0)
            def _():
                arrival(2, first).wait_recv()

            arrival(2, second).wait_recv()
            lefts = []
            for d in (first, second):
                slot = column(d)
                bias = jnp.dot(oht[half * Z + slot], mbuf[...], preferred_element_type=F32)
                left = jnp.concatenate([qbuf[slot], bias.astype(BF16)], axis=1)
                lbuf[slot] = left
                lefts.append(left)
            peak, denom, mixed = weigh(
                jnp.concatenate(lefts, axis=0), half, jnp.full((2 * ROWS, 1), -jnp.inf, F32)
            )
            for i, d in enumerate((first, second)):
                slot = column(d)
                rows = slice(i * ROWS, (i + 1) * ROWS)
                peaks[slot] = peak[rows]
                denoms[slot] = denom[rows]
                mixes[slot] = mixed[rows]
            return carry

        def far_half(t, carry):
            slots = (column(4 + t), column(3 - t))
            left = jnp.concatenate([lbuf[slot] for slot in slots], axis=0)
            before = jnp.concatenate([peaks[slot] for slot in slots], axis=0)
            peak, denom, mixed = weigh(left, 1 - half, before)
            fade = jnp.exp2((before - peak) * factor)
            denom = denom + fade * jnp.concatenate([denoms[slot] for slot in slots], axis=0)
            mixed = mixed + fade * jnp.concatenate([mixes[slot] for slot in slots], axis=0)
            out = (mixed / denom).astype(BF16)
            for i, slot in enumerate(slots):
                obuf[slot] = out[i * ROWS : (i + 1) * ROWS]
            result(slots[0]).start()

            @pl.when(t < 3)
            def _():
                result(slots[1]).start()

            return carry

        lax.fori_loop(0, Z // 2, near_half, 0)
        for kind in range(2):
            for d in FAR_FIRST:
                forward(kind, column(d), 1 - half).wait_recv()
        lax.fori_loop(0, Z // 2, far_half, 0)
        own_result().start()

    for d in range(1, GROUP):
        sum_copy(d).wait_send()
    to_all(lambda d: order_piece(d).wait_send())
    for kind in range(3):
        to_all(lambda d, kind=kind: piece(kind, d).wait_send())

    @pl.when(busy)
    def _():
        order_forward(half).wait_send()
        for kind in range(2):
            for d in FAR_FIRST:
                forward(kind, column(d), half).wait_send()
        for d in FAR_FIRST[:-1]:
            result(column(d)).wait_send()
        own_result().wait()

    to_all(lambda d: result_arrival(d).wait_recv())


def local(query, key, value, q_gain, k_gain, order, cluster_rows, block_map):
    streams = query.shape[0]
    any_ = pl.BlockSpec(memory_space=pl.ANY)
    sems = pltpu.SemaphoreType.DMA
    return pl.pallas_call(
        kernel,
        out_shape=pltpu.VMEM((streams, ROWS, ROWS), BF16),
        in_specs=[any_] * 8,
        out_specs=pl.BlockSpec(memory_space=pltpu.VMEM),
        scratch_shapes=[
            pltpu.VMEM((HEADS, ROWS), F32),
            pltpu.VMEM((HEADS, ROWS), F32),
            pltpu.VMEM((STREAMS, ROWS), jnp.int32),
            pltpu.SMEM((STREAMS, CLUSTERS), jnp.int32),
            pltpu.VMEM((STREAMS, BLOCKS, BLOCKS), jnp.int32),
            pltpu.VMEM((STREAMS, ROWS, ROWS), BF16),
            pltpu.VMEM((STREAMS, ROWS, ROWS), BF16),
            pltpu.VMEM((STREAMS, ROWS, ROWS), BF16),
            pltpu.VMEM((STREAMS, ROWS, ROWS), BF16),
            pltpu.VMEM((8, ROWS), F32),
            pltpu.VMEM((GROUP, 8, ROWS), F32),
            pltpu.VMEM((STREAMS, 8, ROWS), jnp.int32),
            pltpu.VMEM((2, Z, 8, ROWS), jnp.int32),
            pltpu.VMEM((2 * Z, ROWS, ROWS), BF16),
            pltpu.VMEM((2 * Z, ROWS, ROWS), BF16),
            pltpu.VMEM((Z, ROWS, ROWS), BF16),
            pltpu.VMEM((Z, ROWS, ROWS), BF16),
            pltpu.VMEM((2 * Z, ROWS, ROWS), BF16),
            pltpu.VMEM((ROWS, ROWS), BF16),
            pltpu.VMEM((Z, ROWS, 2 * ROWS), BF16),
            pltpu.VMEM((Z, ROWS, 1), F32),
            pltpu.VMEM((Z, ROWS, 1), F32),
            pltpu.VMEM((Z, ROWS, ROWS), F32),
            pltpu.VMEM((2 * ROWS, Z * ROWS), F32),
            pltpu.VMEM((ROWS, 2 * Z * ROWS), BF16),
            pltpu.VMEM((CLUSTERS, 2 * Z * ROWS), BF16),
            sems((7,)),
            sems((GROUP - 1,)),
            sems((GROUP,)),
            sems((Z,)),
            sems((Z,)),
            sems((3, Z)),
            sems((3, Z)),
            sems((2, Z)),
            sems((2, Z)),
            sems((1,)),
            sems((1,)),
            sems((Z,)),
            sems((STREAMS,)),
        ],
        compiler_params=pltpu.CompilerParams(collective_id=0, has_side_effects=True),
        name="attend",
    )(query, key, value, q_gain, k_gain, order, cluster_rows, block_map)


def solution(mesh):
    return jax.shard_map(
        local,
        mesh=mesh,
        in_specs=(
            P("head", "seq", None),
            P("head", "seq", None),
            P("head", "seq", None),
            P(),
            P(),
            P("head", "seq"),
            P("head", None),
            P("head", None, None),
        ),
        out_specs=P("head", "seq", None),
        check_vma=False,
    )
```

```python
import math

import jax
import jax.numpy as jnp
from jax import lax
from jax.experimental import pallas as pl
from jax.experimental.pallas import tpu as pltpu
from jax.sharding import PartitionSpec as P

MESH = pl.DeviceIdType.MESH
F32 = jnp.float32
BF16 = jnp.bfloat16

EPS = 1e-06
ROWS = 128
Z = 8
STREAMS = 5
HEADS = 40
GROUP = 8
CLUSTERS = 16
BLOCKS = 32
MASKED = -(2.0**30)
FAR_FIRST = (4, 3, 5, 2, 6, 1, 7, 0)
KEY_CHUNK = 512
PER = KEY_CHUNK // ROWS
PARTS = Z // PER


def owner_of(z, shift, core):
    v = lax.rem(z - shift + 3 * core + 16, Z)
    stream = jnp.minimum(v - 3 * core * (v // 7), STREAMS - 1)
    busy = jnp.logical_or(v < STREAMS - core, core * v == 7)
    return stream, busy


def kernel(
    q_hbm, k_hbm, v_hbm, qg_hbm, kg_hbm, order_hbm, rows_hbm, map_hbm, out_ref,
    qg_ref, kg_ref, order_ref, rows_ref, map_ref, qraw, kraw, qn, kn, sum_out, sum_in, ord_out, ord_in, kbuf, vbuf, qbuf, obuf,
    oht, mbuf, lbuf, peaks, denoms, mixes, s_scr, bt_scr, a_scr,
    raw_sem, sum_send, sum_recv, ord_send, ord_recv, kv_send, kv_recv, fwd_send, fwd_recv,
    ofw_send, ofw_recv, out_send, out_recv,
):
    me = lax.axis_index("seq")
    head = lax.axis_index("head")
    half, z = me // Z, lax.rem(me, Z)
    shift = 2 * lax.rem(head // 2, 2)
    core = lax.rem(head, 2)
    member = lax.rem(head, GROUP)
    video = head - member
    mine, busy = owner_of(z, shift, core)
    partner = {"seq": (1 - half) * Z + z}

    def column(d):
        return lax.rem(z + d, Z)

    barrier = pltpu.get_barrier_semaphore()
    for d in range(1, Z):
        pl.semaphore_signal(
            barrier, inc=1, device_id={"seq": half * Z + column(d)}, device_id_type=MESH
        )
        pl.semaphore_signal(
            barrier,
            inc=1,
            device_id={"head": video + lax.rem(member + d, GROUP)},
            device_id_type=MESH,
        )
    pl.semaphore_signal(barrier, inc=1, device_id=partner, device_id_type=MESH)

    q_in = pltpu.make_async_copy(q_hbm, qraw, raw_sem.at[0])
    k_in = pltpu.make_async_copy(k_hbm, kraw, raw_sem.at[1])
    small = [
        pltpu.make_async_copy(src, dst, raw_sem.at[2 + i])
        for i, (src, dst) in enumerate(
            (
                (order_hbm, order_ref),
                (kg_hbm, kg_ref),
                (qg_hbm, qg_ref),
                (rows_hbm, rows_ref),
                (map_hbm, map_ref),
            )
        )
    ]
    small[0].start()
    q_in.start()
    k_in.start()
    for copy in small[1:]:
        copy.start()
    def squares(raw):
        total = jnp.zeros((ROWS, ROWS), F32)
        for j in range(STREAMS):
            x = raw[j].astype(F32)
            total = total + x * x
        return jnp.sum(total.T, axis=0, keepdims=True)

    sum_out[...] = jnp.zeros((8, ROWS), F32)
    q_in.wait()
    sum_out[pl.ds(0, 1), :] = squares(qraw)
    k_in.wait()
    sum_out[pl.ds(1, 1), :] = squares(kraw)
    small[0].wait()
    for j in range(STREAMS):
        ord_out[j] = jnp.broadcast_to(order_ref[pl.ds(j, 1), :], (8, ROWS))

    pl.semaphore_wait(barrier, 2 * (Z - 1) + 1)

    def sum_copy(d):
        return pltpu.make_async_remote_copy(
            src_ref=sum_out,
            dst_ref=sum_in.at[member],
            send_sem=sum_send.at[d - 1],
            recv_sem=sum_recv.at[member],
            device_id={"head": video + lax.rem(member + d, GROUP)},
            device_id_type=MESH,
        )

    def sum_arrival(d):
        slot = lax.rem(member + d, GROUP)
        return pltpu.make_async_remote_copy(
            src_ref=sum_out,
            dst_ref=sum_in.at[slot],
            send_sem=sum_send.at[d - 1],
            recv_sem=sum_recv.at[slot],
            device_id={"head": video + slot},
            device_id_type=MESH,
        )

    def piece(kind, d):
        to = column(d)
        stream, _ = owner_of(to, shift, core)
        src = (v_hbm, kn, qn)[kind].at[stream]
        dst = (vbuf.at[me], kbuf.at[me], qbuf.at[z])[kind]
        return pltpu.make_async_remote_copy(
            src_ref=src,
            dst_ref=dst,
            send_sem=kv_send.at[kind, d],
            recv_sem=kv_recv.at[kind, z],
            device_id={"seq": half * Z + to},
            device_id_type=MESH,
        )

    def own_piece(kind):
        src = (v_hbm, kn, qn)[kind].at[mine]
        dst = (vbuf.at[me], kbuf.at[me], qbuf.at[z])[kind]
        return pltpu.make_async_copy(src, dst, kv_recv.at[kind, z])

    def arrival(kind, d):
        slot = column(d)
        dst = (vbuf.at[half * Z + slot], kbuf.at[half * Z + slot], qbuf.at[slot])[kind]
        return pltpu.make_async_remote_copy(
            src_ref=dst,
            dst_ref=dst,
            send_sem=kv_send.at[kind, d],
            recv_sem=kv_recv.at[kind, slot],
            device_id={"seq": half * Z + slot},
            device_id_type=MESH,
        )

    def order_piece(d):
        to = column(d)
        stream, _ = owner_of(to, shift, core)
        return pltpu.make_async_remote_copy(
            src_ref=ord_out.at[stream],
            dst_ref=ord_in.at[half, z],
            send_sem=ord_send.at[d],
            recv_sem=ord_recv.at[z],
            device_id={"seq": half * Z + to},
            device_id_type=MESH,
        )

    def own_order():
        return pltpu.make_async_copy(ord_out.at[mine], ord_in.at[half, z], ord_recv.at[z])

    def order_arrival(d):
        slot = column(d)
        return pltpu.make_async_remote_copy(
            src_ref=ord_in.at[half, slot],
            dst_ref=ord_in.at[half, slot],
            send_sem=ord_send.at[d],
            recv_sem=ord_recv.at[slot],
            device_id={"seq": half * Z + slot},
            device_id_type=MESH,
        )

    def forward(kind, slot, side):
        buf = (vbuf, kbuf)[kind]
        return pltpu.make_async_remote_copy(
            src_ref=buf.at[side * Z + slot],
            dst_ref=buf.at[side * Z + slot],
            send_sem=fwd_send.at[kind, slot],
            recv_sem=fwd_recv.at[kind, slot],
            device_id=partner,
            device_id_type=MESH,
        )

    def order_forward(side):
        return pltpu.make_async_remote_copy(
            src_ref=ord_in.at[side],
            dst_ref=ord_in.at[side],
            send_sem=ofw_send.at[0],
            recv_sem=ofw_recv.at[0],
            device_id=partner,
            device_id_type=MESH,
        )

    def to_all(make):
        for d in FAR_FIRST[:-1]:
            _, there = owner_of(column(d), shift, core)

            @pl.when(there)
            def _(d=d):
                make(d)

    for d in range(1, GROUP):
        sum_copy(d).start()
    to_all(lambda d: order_piece(d).start())
    to_all(lambda d: piece(0, d).start())

    @pl.when(busy)
    def _():
        own_order().start()
        own_piece(0).start()

    for copy in small[1:]:
        copy.wait()
    total = sum_out[...]
    for d in range(1, GROUP):
        sum_arrival(d).wait_recv()
    for d in range(1, GROUP):
        total = total + sum_in[lax.rem(member + d, GROUP)]
    scale = lax.rsqrt(total * (1.0 / (HEADS * ROWS)) + EPS)

    def by_row(row):
        return jnp.broadcast_to(scale[row : row + 1, :], (ROWS, ROWS)).T

    def normalize(kind, d, rows):
        stream, _ = owner_of(column(d), shift, core)
        raw, gains, out = ((kraw, kg_ref, kn), (qraw, qg_ref, qn))[kind - 1]
        gain = gains[pl.ds(member * STREAMS + stream, 1), :]
        out[stream] = (raw[stream].astype(F32) * rows * gain).astype(BF16)

    for kind in (1, 2):
        rows = by_row(2 - kind)

        def ready(d, kind=kind, rows=rows):
            normalize(kind, d, rows)
            piece(kind, d).start()

        to_all(ready)

        @pl.when(busy)
        def _(kind=kind, rows=rows):
            normalize(kind, 0, rows)
            own_piece(kind).start()

    def result(slot):
        return pltpu.make_async_remote_copy(
            src_ref=obuf.at[slot],
            dst_ref=out_ref.at[mine],
            send_sem=out_send.at[slot],
            recv_sem=out_recv.at[mine],
            device_id={"seq": half * Z + slot},
            device_id_type=MESH,
        )

    def own_result():
        return pltpu.make_async_copy(obuf.at[z], out_ref.at[mine], out_recv.at[mine])

    def result_arrival(d):
        stream, _ = owner_of(column(d), shift, core)
        return pltpu.make_async_remote_copy(
            src_ref=obuf.at[0],
            dst_ref=out_ref.at[stream],
            send_sem=out_send.at[0],
            recv_sem=out_recv.at[stream],
            device_id={"seq": half * Z + column(d)},
            device_id_type=MESH,
        )

    @pl.when(busy)
    def _():
        own_order().wait()
        for d in FAR_FIRST[:-1]:
            order_arrival(d).wait_recv()
        order_forward(half).start()
        own_piece(0).wait()
        forward(0, z, half).start()
        for d in FAR_FIRST[:-1]:
            arrival(0, d).wait_recv()
            forward(0, column(d), half).start()
        own_piece(1).wait()
        forward(1, z, half).start()
        for d in FAR_FIRST[:4]:
            arrival(1, d).wait_recv()
            forward(1, column(d), half).start()

        order_forward(1 - half).wait_recv()
        tokens = ord_in[:, :, 0, :].reshape(CLUSTERS, ROWS)
        place = lax.broadcasted_iota(jnp.int32, (CLUSTERS, ROWS), 0) * ROWS
        place = place + lax.broadcasted_iota(jnp.int32, (CLUSTERS, ROWS), 1)
        owner = jnp.full((CLUSTERS, ROWS), -1, jnp.int32)
        start = jnp.zeros((CLUSTERS, ROWS), jnp.int32)
        at = jnp.int32(0)
        for o in range(CLUSTERS):
            begun = place >= at
            owner = owner + begun.astype(jnp.int32)
            start = jnp.where(begun, at, start)
            at = at + rows_ref[mine, o]
        block = (owner * 2 + jnp.right_shift(place - start, 7)).astype(F32)
        high = jnp.right_shift(tokens, 7)
        low = jnp.bitwise_and(tokens, ROWS - 1)
        digit = lax.broadcasted_iota(jnp.int32, (ROWS, ROWS), 0)
        digit_high = lax.broadcasted_iota(jnp.int32, (CLUSTERS, ROWS), 0)
        for i in range(CLUSTERS):
            span = pl.ds(i * ROWS, ROWS)
            hit = digit == jnp.broadcast_to(low[i : i + 1], (ROWS, ROWS))
            bt_scr[:, span] = jnp.where(hit, 1.0, 0.0).astype(BF16)
            hit = digit_high == jnp.broadcast_to(high[i : i + 1], (CLUSTERS, ROWS))
            here = jnp.broadcast_to(block[i : i + 1], (CLUSTERS, ROWS))
            a_scr[:, span] = jnp.where(hit, here, 0.0).astype(BF16)
        by_low = lax.dot_general(
            bt_scr[...], a_scr[...], (((1,), (1,)), ((), ())), preferred_element_type=F32
        ).astype(BF16)
        lane = lax.broadcasted_iota(jnp.int32, (CLUSTERS, ROWS * CLUSTERS), 1)
        spread = jnp.right_shift(lane, 7) == lax.broadcasted_iota(
            jnp.int32, (CLUSTERS, ROWS * CLUSTERS), 0
        )
        wide = jnp.dot(
            by_low, jnp.where(spread, 1.0, 0.0).astype(BF16), preferred_element_type=F32
        )
        which = lax.broadcasted_iota(jnp.int32, (ROWS, ROWS), 1).astype(F32)
        for i in range(CLUSTERS):
            hit = wide[:, i * ROWS : (i + 1) * ROWS] == which
            oht[i] = jnp.where(hit, 1.0, 0.0).astype(BF16)
        mbuf[...] = jnp.zeros((ROWS, ROWS), BF16)
        same = lax.broadcasted_iota(jnp.int32, (BLOCKS, BLOCKS), 0) == (
            lax.broadcasted_iota(jnp.int32, (BLOCKS, BLOCKS), 1)
        )
        open_ = jnp.logical_or(map_ref[mine] == 1, same)
        mbuf[pl.ds(0, BLOCKS), pl.ds(0, BLOCKS)] = jnp.where(open_, 0.0, MASKED).astype(BF16)

        for d in FAR_FIRST[4:-1]:
            arrival(1, d).wait_recv()
            forward(1, column(d), half).start()

        factor = math.log2(math.e) / math.sqrt(ROWS)

        def weigh(left, side, start):
            peak = start
            for i in range(PARTS):
                span = pl.ds(side * Z + i * PER, PER)
                scores = lax.dot_general(
                    left,
                    jnp.concatenate(
                        [
                            kbuf[span].reshape(KEY_CHUNK, ROWS),
                            oht[span].reshape(KEY_CHUNK, ROWS),
                        ],
                        axis=1,
                    ),
                    (((1,), (1,)), ((), ())),
                    preferred_element_type=F32,
                )
                s_scr[:, pl.ds(i * KEY_CHUNK, KEY_CHUNK)] = scores
                peak = jnp.maximum(peak, jnp.max(scores, axis=1, keepdims=True))
            denom = jnp.zeros((2 * ROWS, 1), F32)
            mixed = jnp.zeros((2 * ROWS, ROWS), F32)
            for i in range(PARTS):
                span = pl.ds(side * Z + i * PER, PER)
                p = jnp.exp2((s_scr[:, pl.ds(i * KEY_CHUNK, KEY_CHUNK)] - peak) * factor)
                denom = denom + jnp.sum(p, axis=1, keepdims=True)
                values = vbuf[span].reshape(KEY_CHUNK, ROWS)
                mixed = mixed + jnp.dot(p.astype(BF16), values, preferred_element_type=F32)
            return peak, denom, mixed

        def near_half(t):
            first, second = 4 + t, 3 - t
            arrival(2, first).wait_recv()

            @pl.when(t < 3)
            def _():
                arrival(2, second).wait_recv()

            @pl.when(t == 3)
            def _():
                own_piece(2).wait()

            lefts = []
            for d in (first, second):
                slot = column(d)
                bias = jnp.dot(oht[half * Z + slot], mbuf[...], preferred_element_type=F32)
                left = jnp.concatenate([qbuf[slot], bias.astype(BF16)], axis=1)
                lbuf[slot] = left
                lefts.append(left)
            peak, denom, mixed = weigh(
                jnp.concatenate(lefts, axis=0), half, jnp.full((2 * ROWS, 1), -jnp.inf, F32)
            )
            for i, d in enumerate((first, second)):
                slot = column(d)
                rows = slice(i * ROWS, (i + 1) * ROWS)
                peaks[slot] = peak[rows]
                denoms[slot] = denom[rows]
                mixes[slot] = mixed[rows]

        def far_half(t):
            slots = (column(4 + t), column(3 - t))
            left = jnp.concatenate([lbuf[slot] for slot in slots], axis=0)
            before = jnp.concatenate([peaks[slot] for slot in slots], axis=0)
            peak, denom, mixed = weigh(left, 1 - half, before)
            fade = jnp.exp2((before - peak) * factor)
            denom = denom + fade * jnp.concatenate([denoms[slot] for slot in slots], axis=0)
            mixed = mixed + fade * jnp.concatenate([mixes[slot] for slot in slots], axis=0)
            out = (mixed / denom).astype(BF16)
            for i, slot in enumerate(slots):
                obuf[slot] = out[i * ROWS : (i + 1) * ROWS]
            result(slots[0]).start()

            @pl.when(t < 3)
            def _():
                result(slots[1]).start()

            @pl.when(t == 3)
            def _():
                own_result().start()

        def step(i, carry):
            near = jnp.logical_or(i < 3, i == 5)

            @pl.when(near)
            def _():
                near_half(jnp.minimum(i, 3))

            @pl.when(i == 3)
            def _():
                for kind in range(2):
                    for d in FAR_FIRST:
                        forward(kind, column(d), 1 - half).wait_recv()

            @pl.when(jnp.logical_not(near))
            def _():
                far_half(i - 3 - i // 6)

            return carry

        lax.fori_loop(0, Z, step, 0)

    for d in range(1, GROUP):
        sum_copy(d).wait_send()
    to_all(lambda d: order_piece(d).wait_send())
    for kind in range(3):
        to_all(lambda d, kind=kind: piece(kind, d).wait_send())

    @pl.when(busy)
    def _():
        order_forward(half).wait_send()
        for kind in range(2):
            for d in FAR_FIRST:
                forward(kind, column(d), half).wait_send()
        for d in FAR_FIRST[:-1]:
            result(column(d)).wait_send()
        own_result().wait()

    to_all(lambda d: result_arrival(d).wait_recv())


def local(query, key, value, q_gain, k_gain, order, cluster_rows, block_map):
    streams = query.shape[0]
    any_ = pl.BlockSpec(memory_space=pl.ANY)
    sems = pltpu.SemaphoreType.DMA
    return pl.pallas_call(
        kernel,
        out_shape=pltpu.VMEM((streams, ROWS, ROWS), BF16),
        in_specs=[any_] * 8,
        out_specs=pl.BlockSpec(memory_space=pltpu.VMEM),
        scratch_shapes=[
            pltpu.VMEM((HEADS, ROWS), F32),
            pltpu.VMEM((HEADS, ROWS), F32),
            pltpu.VMEM((STREAMS, ROWS), jnp.int32),
            pltpu.SMEM((STREAMS, CLUSTERS), jnp.int32),
            pltpu.VMEM((STREAMS, BLOCKS, BLOCKS), jnp.int32),
            pltpu.VMEM((STREAMS, ROWS, ROWS), BF16),
            pltpu.VMEM((STREAMS, ROWS, ROWS), BF16),
            pltpu.VMEM((STREAMS, ROWS, ROWS), BF16),
            pltpu.VMEM((STREAMS, ROWS, ROWS), BF16),
            pltpu.VMEM((8, ROWS), F32),
            pltpu.VMEM((GROUP, 8, ROWS), F32),
            pltpu.VMEM((STREAMS, 8, ROWS), jnp.int32),
            pltpu.VMEM((2, Z, 8, ROWS), jnp.int32),
            pltpu.VMEM((2 * Z, ROWS, ROWS), BF16),
            pltpu.VMEM((2 * Z, ROWS, ROWS), BF16),
            pltpu.VMEM((Z, ROWS, ROWS), BF16),
            pltpu.VMEM((Z, ROWS, ROWS), BF16),
            pltpu.VMEM((2 * Z, ROWS, ROWS), BF16),
            pltpu.VMEM((ROWS, ROWS), BF16),
            pltpu.VMEM((Z, ROWS, 2 * ROWS), BF16),
            pltpu.VMEM((Z, ROWS, 1), F32),
            pltpu.VMEM((Z, ROWS, 1), F32),
            pltpu.VMEM((Z, ROWS, ROWS), F32),
            pltpu.VMEM((2 * ROWS, Z * ROWS), F32),
            pltpu.VMEM((ROWS, 2 * Z * ROWS), BF16),
            pltpu.VMEM((CLUSTERS, 2 * Z * ROWS), BF16),
            sems((7,)),
            sems((GROUP - 1,)),
            sems((GROUP,)),
            sems((Z,)),
            sems((Z,)),
            sems((3, Z)),
            sems((3, Z)),
            sems((2, Z)),
            sems((2, Z)),
            sems((1,)),
            sems((1,)),
            sems((Z,)),
            sems((STREAMS,)),
        ],
        compiler_params=pltpu.CompilerParams(collective_id=0, has_side_effects=True),
        name="attend",
    )(query, key, value, q_gain, k_gain, order, cluster_rows, block_map)


def solution(mesh):
    return jax.shard_map(
        local,
        mesh=mesh,
        in_specs=(
            P("head", "seq", None),
            P("head", "seq", None),
            P("head", "seq", None),
            P(),
            P(),
            P("head", "seq"),
            P("head", None),
            P("head", None, None),
        ),
        out_specs=P("head", "seq", None),
        check_vma=False,
    )
```

```python
import math

import jax
import jax.numpy as jnp
from jax import lax
from jax.experimental import pallas as pl
from jax.experimental.pallas import tpu as pltpu
from jax.sharding import PartitionSpec as P

MESH = pl.DeviceIdType.MESH
F32 = jnp.float32
BF16 = jnp.bfloat16

EPS = 1e-06
ROWS = 128
Z = 8
STREAMS = 5
HEADS = 40
GROUP = 8
CLUSTERS = 16
BLOCKS = 32
MASKED = -(2.0**30)
FAR_FIRST = (4, 3, 5, 2, 6, 1, 7, 0)
KEY_CHUNK = 512
V_FIRST = 2
PER = KEY_CHUNK // ROWS
PARTS = Z // PER


def owner_of(z, shift, core):
    v = lax.rem(z - shift + 3 * core + 16, Z)
    stream = jnp.minimum(v - 3 * core * (v // 7), STREAMS - 1)
    busy = jnp.logical_or(v < STREAMS - core, core * v == 7)
    return stream, busy


def kernel(
    q_hbm, k_hbm, v_hbm, qg_hbm, kg_hbm, order_hbm, rows_hbm, map_hbm, out_ref,
    qg_ref, kg_ref, rows_ref, map_ref, qraw, kraw, qn, kn, sum_out, sum_in, ord_in, kbuf, vbuf, qbuf, obuf,
    oht, mbuf, lbuf, peaks, denoms, mixes, s_scr, s_two, bt_scr, a_scr,
    raw_sem, sum_send, sum_recv, ord_send, ord_recv, kv_send, kv_recv, fwd_send, fwd_recv,
    ofw_send, ofw_recv, out_send, out_recv,
):
    me = lax.axis_index("seq")
    head = lax.axis_index("head")
    half, z = me // Z, lax.rem(me, Z)
    shift = 2 * lax.rem(head // 2, 2)
    core = lax.rem(head, 2)
    member = lax.rem(head, GROUP)
    video = head - member
    mine, busy = owner_of(z, shift, core)
    partner = {"seq": (1 - half) * Z + z}

    def column(d):
        return lax.rem(z + d, Z)

    barrier = pltpu.get_barrier_semaphore()
    for d in range(1, Z):
        pl.semaphore_signal(
            barrier, inc=1, device_id={"seq": half * Z + column(d)}, device_id_type=MESH
        )
        pl.semaphore_signal(
            barrier,
            inc=1,
            device_id={"head": video + lax.rem(member + d, GROUP)},
            device_id_type=MESH,
        )
    pl.semaphore_signal(barrier, inc=1, device_id=partner, device_id_type=MESH)

    q_in = pltpu.make_async_copy(q_hbm, qraw, raw_sem.at[0])
    k_in = pltpu.make_async_copy(k_hbm, kraw, raw_sem.at[1])
    small = [
        pltpu.make_async_copy(src, dst, raw_sem.at[2 + i])
        for i, (src, dst) in enumerate(
            (
                (kg_hbm, kg_ref),
                (qg_hbm, qg_ref),
                (rows_hbm, rows_ref),
                (map_hbm, map_ref),
            )
        )
    ]
    q_in.start()
    k_in.start()
    for copy in small:
        copy.start()
    pl.semaphore_wait(barrier, 2 * (Z - 1) + 1)

    def sum_copy(d):
        return pltpu.make_async_remote_copy(
            src_ref=sum_out,
            dst_ref=sum_in.at[member],
            send_sem=sum_send.at[d - 1],
            recv_sem=sum_recv.at[member],
            device_id={"head": video + lax.rem(member + d, GROUP)},
            device_id_type=MESH,
        )

    def sum_arrival(d):
        slot = lax.rem(member + d, GROUP)
        return pltpu.make_async_remote_copy(
            src_ref=sum_out,
            dst_ref=sum_in.at[slot],
            send_sem=sum_send.at[d - 1],
            recv_sem=sum_recv.at[slot],
            device_id={"head": video + slot},
            device_id_type=MESH,
        )

    def piece(kind, d):
        to = column(d)
        stream, _ = owner_of(to, shift, core)
        src = (v_hbm, kn, qn)[kind].at[stream]
        dst = (vbuf.at[me], kbuf.at[me], qbuf.at[z])[kind]
        return pltpu.make_async_remote_copy(
            src_ref=src,
            dst_ref=dst,
            send_sem=kv_send.at[kind, d],
            recv_sem=kv_recv.at[kind, z],
            device_id={"seq": half * Z + to},
            device_id_type=MESH,
        )

    def own_piece(kind):
        src = (v_hbm, kn, qn)[kind].at[mine]
        dst = (vbuf.at[me], kbuf.at[me], qbuf.at[z])[kind]
        return pltpu.make_async_copy(src, dst, kv_recv.at[kind, z])

    def arrival(kind, d):
        slot = column(d)
        dst = (vbuf.at[half * Z + slot], kbuf.at[half * Z + slot], qbuf.at[slot])[kind]
        return pltpu.make_async_remote_copy(
            src_ref=dst,
            dst_ref=dst,
            send_sem=kv_send.at[kind, d],
            recv_sem=kv_recv.at[kind, slot],
            device_id={"seq": half * Z + slot},
            device_id_type=MESH,
        )

    def order_piece(d):
        to = column(d)
        return pltpu.make_async_remote_copy(
            src_ref=order_hbm,
            dst_ref=ord_in.at[half, z],
            send_sem=ord_send.at[d],
            recv_sem=ord_recv.at[z],
            device_id={"seq": half * Z + to},
            device_id_type=MESH,
        )

    def own_order():
        return pltpu.make_async_copy(order_hbm, ord_in.at[half, z], ord_recv.at[z])

    def order_arrival(d):
        slot = column(d)
        return pltpu.make_async_remote_copy(
            src_ref=ord_in.at[half, slot],
            dst_ref=ord_in.at[half, slot],
            send_sem=ord_send.at[d],
            recv_sem=ord_recv.at[slot],
            device_id={"seq": half * Z + slot},
            device_id_type=MESH,
        )

    def forward(kind, slot, side):
        buf = (vbuf, kbuf)[kind]
        return pltpu.make_async_remote_copy(
            src_ref=buf.at[side * Z + slot],
            dst_ref=buf.at[side * Z + slot],
            send_sem=fwd_send.at[kind, slot],
            recv_sem=fwd_recv.at[kind, slot],
            device_id=partner,
            device_id_type=MESH,
        )

    def own_value():
        return pltpu.make_async_remote_copy(
            src_ref=v_hbm.at[mine],
            dst_ref=vbuf.at[me],
            send_sem=fwd_send.at[0, z],
            recv_sem=fwd_recv.at[0, z],
            device_id=partner,
            device_id_type=MESH,
        )

    def order_forward(side):
        return pltpu.make_async_remote_copy(
            src_ref=ord_in.at[side],
            dst_ref=ord_in.at[side],
            send_sem=ofw_send.at[0],
            recv_sem=ofw_recv.at[0],
            device_id=partner,
            device_id_type=MESH,
        )

    def to_all(make):
        for d in FAR_FIRST[:-1]:
            _, there = owner_of(column(d), shift, core)

            @pl.when(there)
            def _(d=d):
                make(d)

    to_all(lambda d: order_piece(d).start())
    to_all(lambda d: piece(0, d).start())

    @pl.when(busy)
    def _():
        own_value().start()
        own_order().start()
        own_piece(0).start()

    def squares(raw):
        total = jnp.zeros((ROWS, ROWS), F32)
        for j in range(STREAMS):
            x = raw[j].astype(F32)
            total = total + x * x
        return jnp.sum(total.T, axis=0, keepdims=True)

    sum_out[...] = jnp.zeros((8, ROWS), F32)
    q_in.wait()
    sum_out[pl.ds(0, 1), :] = squares(qraw)
    k_in.wait()
    sum_out[pl.ds(1, 1), :] = squares(kraw)
    for d in range(1, GROUP):
        sum_copy(d).start()
    for copy in small:
        copy.wait()
    total = sum_out[...]
    for d in range(1, GROUP):
        sum_arrival(d).wait_recv()
    for d in range(1, GROUP):
        total = total + sum_in[lax.rem(member + d, GROUP)]
    scale = lax.rsqrt(total * (1.0 / (HEADS * ROWS)) + EPS)

    def by_row(row):
        return jnp.broadcast_to(scale[row : row + 1, :], (ROWS, ROWS)).T

    def normalize(kind, d, rows):
        stream, _ = owner_of(column(d), shift, core)
        raw, gains, out = ((kraw, kg_ref, kn), (qraw, qg_ref, qn))[kind - 1]
        gain = gains[pl.ds(member * STREAMS + stream, 1), :]
        out[stream] = (raw[stream].astype(F32) * rows * gain).astype(BF16)

    rows = by_row(1)

    def ready_key(d):
        normalize(1, d, rows)
        piece(1, d).start()

    to_all(ready_key)

    @pl.when(busy)
    def _():
        normalize(1, 0, rows)
        own_piece(1).start()

    rows_q = by_row(0)

    @pl.when(jnp.logical_not(busy))
    def _():
        to_all(lambda d: normalize(2, d, rows_q))
        to_all(lambda d: piece(2, d).start())

    def result(slot):
        return pltpu.make_async_remote_copy(
            src_ref=obuf.at[slot],
            dst_ref=out_ref.at[mine],
            send_sem=out_send.at[slot],
            recv_sem=out_recv.at[mine],
            device_id={"seq": half * Z + slot},
            device_id_type=MESH,
        )

    def own_result():
        return pltpu.make_async_copy(obuf.at[z], out_ref.at[mine], out_recv.at[mine])

    def result_arrival(d):
        stream, _ = owner_of(column(d), shift, core)
        return pltpu.make_async_remote_copy(
            src_ref=obuf.at[0],
            dst_ref=out_ref.at[stream],
            send_sem=out_send.at[0],
            recv_sem=out_recv.at[stream],
            device_id={"seq": half * Z + column(d)},
            device_id_type=MESH,
        )

    @pl.when(busy)
    def _():
        for d in FAR_FIRST[:V_FIRST]:
            arrival(0, d).wait_recv()
            forward(0, column(d), half).start()

        def ready_query(d):
            normalize(2, d, rows_q)
            piece(2, d).start()

        to_all(ready_query)
        normalize(2, 0, rows_q)
        own_piece(2).start()
        own_order().wait()
        for d in FAR_FIRST[:-1]:
            order_arrival(d).wait_recv()
        order_forward(half).start()
        for d in FAR_FIRST[V_FIRST:-1]:
            arrival(0, d).wait_recv()
            forward(0, column(d), half).start()
        own_piece(0).wait()
        own_piece(1).wait()
        forward(1, z, half).start()
        for d in FAR_FIRST[:4]:
            arrival(1, d).wait_recv()
            forward(1, column(d), half).start()

        order_forward(1 - half).wait_recv()
        tokens = ord_in[:, :, pl.ds(mine, 1), :].reshape(CLUSTERS, ROWS)
        place = lax.broadcasted_iota(jnp.int32, (CLUSTERS, ROWS), 0) * ROWS
        place = place + lax.broadcasted_iota(jnp.int32, (CLUSTERS, ROWS), 1)
        owner = jnp.full((CLUSTERS, ROWS), -1, jnp.int32)
        start = jnp.zeros((CLUSTERS, ROWS), jnp.int32)
        at = jnp.int32(0)
        for o in range(CLUSTERS):
            begun = place >= at
            owner = owner + begun.astype(jnp.int32)
            start = jnp.where(begun, at, start)
            at = at + rows_ref[mine, o]
        block = (owner * 2 + jnp.right_shift(place - start, 7)).astype(F32)
        high = jnp.right_shift(tokens, 7)
        low = jnp.bitwise_and(tokens, ROWS - 1)
        digit = lax.broadcasted_iota(jnp.int32, (ROWS, ROWS), 0)
        digit_high = lax.broadcasted_iota(jnp.int32, (CLUSTERS, ROWS), 0)
        for i in range(CLUSTERS):
            span = pl.ds(i * ROWS, ROWS)
            hit = digit == jnp.broadcast_to(low[i : i + 1], (ROWS, ROWS))
            bt_scr[:, span] = jnp.where(hit, 1.0, 0.0).astype(BF16)
            hit = digit_high == jnp.broadcast_to(high[i : i + 1], (CLUSTERS, ROWS))
            here = jnp.broadcast_to(block[i : i + 1], (CLUSTERS, ROWS))
            a_scr[:, span] = jnp.where(hit, here, 0.0).astype(BF16)
        by_low = lax.dot_general(
            bt_scr[...], a_scr[...], (((1,), (1,)), ((), ())), preferred_element_type=F32
        ).astype(BF16)
        lane = lax.broadcasted_iota(jnp.int32, (CLUSTERS, ROWS * CLUSTERS), 1)
        spread = jnp.right_shift(lane, 7) == lax.broadcasted_iota(
            jnp.int32, (CLUSTERS, ROWS * CLUSTERS), 0
        )
        wide = jnp.dot(
            by_low, jnp.where(spread, 1.0, 0.0).astype(BF16), preferred_element_type=F32
        )
        which = lax.broadcasted_iota(jnp.int32, (ROWS, ROWS), 1).astype(F32)
        for i in range(CLUSTERS):
            hit = wide[:, i * ROWS : (i + 1) * ROWS] == which
            oht[i] = jnp.where(hit, 1.0, 0.0).astype(BF16)
        mbuf[...] = jnp.zeros((ROWS, ROWS), BF16)
        same = lax.broadcasted_iota(jnp.int32, (BLOCKS, BLOCKS), 0) == (
            lax.broadcasted_iota(jnp.int32, (BLOCKS, BLOCKS), 1)
        )
        open_ = jnp.logical_or(map_ref[mine] == 1, same)
        mbuf[pl.ds(0, BLOCKS), pl.ds(0, BLOCKS)] = jnp.where(open_, 0.0, MASKED).astype(BF16)

        for d in FAR_FIRST[4:-1]:
            arrival(1, d).wait_recv()
            forward(1, column(d), half).start()

        factor = math.log2(math.e) / math.sqrt(ROWS)

        def score(left, side, start, into):
            peak = start
            for i in range(PARTS):
                span = pl.ds(side * Z + i * PER, PER)
                keys = kbuf[span].reshape(KEY_CHUNK, ROWS)
                tags = oht[span].reshape(KEY_CHUNK, ROWS)
                scores = lax.dot_general(
                    left,
                    jnp.concatenate([keys, tags], axis=1),
                    (((1,), (1,)), ((), ())),
                    preferred_element_type=F32,
                )
                into[:, pl.ds(i * KEY_CHUNK, KEY_CHUNK)] = scores
                peak = jnp.maximum(peak, jnp.max(scores, axis=1, keepdims=True))
            return peak

        def mix(peak, side, held):
            denom = jnp.zeros((2 * ROWS, 1), F32)
            mixed = jnp.zeros((2 * ROWS, ROWS), F32)
            for i in range(PARTS):
                span = pl.ds(side * Z + i * PER, PER)
                p = jnp.exp2((held[:, pl.ds(i * KEY_CHUNK, KEY_CHUNK)] - peak) * factor)
                denom = denom + jnp.sum(p, axis=1, keepdims=True)
                values = vbuf[span].reshape(KEY_CHUNK, ROWS)
                mixed = mixed + jnp.dot(p.astype(BF16), values, preferred_element_type=F32)
            return denom, mixed

        def near_half(t, carry):
            first, second = 4 + t, 3 - t
            arrival(2, first).wait_recv()

            @pl.when(t < 3)
            def _():
                arrival(2, second).wait_recv()

            @pl.when(t == 3)
            def _():
                own_piece(2).wait()

            lefts = []
            for d in (first, second):
                slot = column(d)
                bias = jnp.dot(oht[half * Z + slot], mbuf[...], preferred_element_type=F32)
                left = jnp.concatenate([qbuf[slot], bias.astype(BF16)], axis=1)
                lbuf[slot] = left
                lefts.append(left)
            start = jnp.full((2 * ROWS, 1), -jnp.inf, F32)
            peak = score(jnp.concatenate(lefts, axis=0), half, start, s_scr)
            denom, mixed = mix(peak, half, s_scr)
            for i, d in enumerate((first, second)):
                slot = column(d)
                rows = slice(i * ROWS, (i + 1) * ROWS)
                peaks[slot] = peak[rows]
                denoms[slot] = denom[rows]
                mixes[slot] = mixed[rows]
            return carry

        lax.fori_loop(0, Z // 2, near_half, 0)
        for kind in range(2):
            for d in FAR_FIRST:
                forward(kind, column(d), 1 - half).wait_recv()

        def far_score(t):
            slots = (column(4 + t), column(3 - t))
            left = jnp.concatenate([lbuf[slot] for slot in slots], axis=0)
            before = jnp.concatenate([peaks[slot] for slot in slots], axis=0)
            return before, score(left, 1 - half, before, (s_scr, s_two)[t % 2])

        def far_mix(t, before, peak):
            slots = (column(4 + t), column(3 - t))
            denom, mixed = mix(peak, 1 - half, (s_scr, s_two)[t % 2])
            fade = jnp.exp2((before - peak) * factor)
            denom = denom + fade * jnp.concatenate([denoms[slot] for slot in slots], axis=0)
            mixed = mixed + fade * jnp.concatenate([mixes[slot] for slot in slots], axis=0)
            out = (mixed / denom).astype(BF16)
            for i, slot in enumerate(slots):
                obuf[slot] = out[i * ROWS : (i + 1) * ROWS]

        held = far_score(0)
        for t in range(Z // 2):
            ahead = far_score(t + 1) if t < 3 else None
            far_mix(t, *held)
            held = ahead
            result(column(4 + t)).start()
            if t < 3:
                result(column(3 - t)).start()
        own_result().start()

    for d in range(1, GROUP):
        sum_copy(d).wait_send()
    to_all(lambda d: order_piece(d).wait_send())
    for kind in range(3):
        to_all(lambda d, kind=kind: piece(kind, d).wait_send())

    @pl.when(busy)
    def _():
        order_forward(half).wait_send()
        for kind in range(2):
            for d in FAR_FIRST:
                forward(kind, column(d), half).wait_send()
        for d in FAR_FIRST[:-1]:
            result(column(d)).wait_send()
        own_result().wait()

    to_all(lambda d: result_arrival(d).wait_recv())


def local(query, key, value, q_gain, k_gain, order, cluster_rows, block_map):
    streams = query.shape[0]
    any_ = pl.BlockSpec(memory_space=pl.ANY)
    sems = pltpu.SemaphoreType.DMA
    return pl.pallas_call(
        kernel,
        out_shape=pltpu.VMEM((streams, ROWS, ROWS), BF16),
        in_specs=[any_] * 8,
        out_specs=pl.BlockSpec(memory_space=pltpu.VMEM),
        scratch_shapes=[
            pltpu.VMEM((HEADS, ROWS), F32),
            pltpu.VMEM((HEADS, ROWS), F32),
            pltpu.SMEM((STREAMS, CLUSTERS), jnp.int32),
            pltpu.VMEM((STREAMS, BLOCKS, BLOCKS), jnp.int32),
            pltpu.VMEM((STREAMS, ROWS, ROWS), BF16),
            pltpu.VMEM((STREAMS, ROWS, ROWS), BF16),
            pltpu.VMEM((STREAMS, ROWS, ROWS), BF16),
            pltpu.VMEM((STREAMS, ROWS, ROWS), BF16),
            pltpu.VMEM((8, ROWS), F32),
            pltpu.VMEM((GROUP, 8, ROWS), F32),
            pltpu.VMEM((2, Z, STREAMS, ROWS), jnp.int32),
            pltpu.VMEM((2 * Z, ROWS, ROWS), BF16),
            pltpu.VMEM((2 * Z, ROWS, ROWS), BF16),
            pltpu.VMEM((Z, ROWS, ROWS), BF16),
            pltpu.VMEM((Z, ROWS, ROWS), BF16),
            pltpu.VMEM((2 * Z, ROWS, ROWS), BF16),
            pltpu.VMEM((ROWS, ROWS), BF16),
            pltpu.VMEM((Z, ROWS, 2 * ROWS), BF16),
            pltpu.VMEM((Z, ROWS, 1), F32),
            pltpu.VMEM((Z, ROWS, 1), F32),
            pltpu.VMEM((Z, ROWS, ROWS), F32),
            pltpu.VMEM((2 * ROWS, Z * ROWS), F32),
            pltpu.VMEM((2 * ROWS, Z * ROWS), F32),
            pltpu.VMEM((ROWS, 2 * Z * ROWS), BF16),
            pltpu.VMEM((CLUSTERS, 2 * Z * ROWS), BF16),
            sems((6,)),
            sems((GROUP - 1,)),
            sems((GROUP,)),
            sems((Z,)),
            sems((Z,)),
            sems((3, Z)),
            sems((3, Z)),
            sems((2, Z)),
            sems((2, Z)),
            sems((1,)),
            sems((1,)),
            sems((Z,)),
            sems((STREAMS,)),
        ],
        compiler_params=pltpu.CompilerParams(collective_id=0, has_side_effects=True),
        name="attend",
    )(query, key, value, q_gain, k_gain, order, cluster_rows, block_map)


def solution(mesh):
    return jax.shard_map(
        local,
        mesh=mesh,
        in_specs=(
            P("head", "seq", None),
            P("head", "seq", None),
            P("head", "seq", None),
            P(),
            P(),
            P("head", "seq"),
            P("head", None),
            P("head", None, None),
        ),
        out_specs=P("head", "seq", None),
        check_vma=False,
    )
```

```python
import math

import jax
import jax.numpy as jnp
from jax import lax
from jax.experimental import pallas as pl
from jax.experimental.pallas import tpu as pltpu
from jax.sharding import PartitionSpec as P

MESH = pl.DeviceIdType.MESH
F32 = jnp.float32
BF16 = jnp.bfloat16

EPS = 1e-06
ROWS = 128
Z = 8
STREAMS = 5
HEADS = 40
GROUP = 8
CLUSTERS = 16
BLOCKS = 32
MASKED = -(2.0**30)
FAR_FIRST = (4, 3, 5, 2, 6, 1, 7, 0)
KEY_CHUNK = 512
V_FIRST = 2
PER = KEY_CHUNK // ROWS
PARTS = Z // PER


def owner_of(z, shift, core):
    v = lax.rem(z - shift + 3 * core + 16, Z)
    stream = jnp.minimum(v - 3 * core * (v // 7), STREAMS - 1)
    busy = jnp.logical_or(v < STREAMS - core, core * v == 7)
    return stream, busy


def pair_of(d):
    return d - 4 if d >= 4 else 3 - d


def kernel(
    q_hbm, k_hbm, v_hbm, qg_hbm, kg_hbm, order_hbm, rows_hbm, map_hbm, out_ref,
    qg_ref, kg_ref, rows_ref, map_ref, qraw, kraw, qn, kn, sum_out, sum_in, ord_in, kbuf, vbuf, qbuf, obuf,
    oht, mbuf, lbuf, peaks, denoms, mixes, s_scr, s_two, bt_scr, a_scr,
    raw_sem, own_sem, sum_send, sum_recv, ord_send, ord_recv, kv_send, kv_recv, q_recv, fwd_send, fwd_recv,
    ofw_send, ofw_recv, out_send, out_recv,
):
    me = lax.axis_index("seq")
    head = lax.axis_index("head")
    half, z = me // Z, lax.rem(me, Z)
    shift = 2 * lax.rem(head // 2, 2)
    core = lax.rem(head, 2)
    member = lax.rem(head, GROUP)
    video = head - member
    mine, busy = owner_of(z, shift, core)
    partner = {"seq": (1 - half) * Z + z}

    def column(d):
        return lax.rem(z + d, Z)

    barrier = pltpu.get_barrier_semaphore()
    for d in range(1, Z):
        pl.semaphore_signal(
            barrier, inc=1, device_id={"seq": half * Z + column(d)}, device_id_type=MESH
        )
        pl.semaphore_signal(
            barrier,
            inc=1,
            device_id={"head": video + lax.rem(member + d, GROUP)},
            device_id_type=MESH,
        )
    pl.semaphore_signal(barrier, inc=1, device_id=partner, device_id_type=MESH)

    q_in = pltpu.make_async_copy(q_hbm, qraw, raw_sem.at[0])
    k_in = pltpu.make_async_copy(k_hbm, kraw, raw_sem.at[1])
    small = [
        pltpu.make_async_copy(src, dst, raw_sem.at[2 + i])
        for i, (src, dst) in enumerate(
            (
                (kg_hbm, kg_ref),
                (qg_hbm, qg_ref),
                (rows_hbm, rows_ref),
                (map_hbm, map_ref),
            )
        )
    ]
    q_in.start()
    k_in.start()
    for copy in small:
        copy.start()
    pl.semaphore_wait(barrier, 2 * (Z - 1) + 1)

    def sum_copy(d):
        return pltpu.make_async_remote_copy(
            src_ref=sum_out,
            dst_ref=sum_in.at[member],
            send_sem=sum_send.at[0],
            recv_sem=sum_recv.at[0],
            device_id={"head": video + lax.rem(member + d, GROUP)},
            device_id_type=MESH,
        )

    def waiting(ref, send_sem, recv_sem):
        return pltpu.make_async_remote_copy(
            src_ref=ref,
            dst_ref=ref,
            send_sem=send_sem,
            recv_sem=recv_sem,
            device_id=partner,
            device_id_type=MESH,
        )

    all_sums = waiting(sum_in.at[pl.ds(0, GROUP - 1)], sum_send.at[0], sum_recv.at[0])

    def piece(kind, d):
        to = column(d)
        stream, _ = owner_of(to, shift, core)
        src = (v_hbm, kn, qn)[kind].at[stream]
        dst = (vbuf.at[me], kbuf.at[me], qbuf.at[z])[kind]
        return pltpu.make_async_remote_copy(
            src_ref=src,
            dst_ref=dst,
            send_sem=kv_send.at[0],
            recv_sem=q_recv.at[pair_of(Z - d)] if kind == 2 else kv_recv.at[kind, z],
            device_id={"seq": half * Z + to},
            device_id_type=MESH,
        )

    def own_piece(kind):
        src = (v_hbm, kn, qn)[kind].at[mine]
        dst = (vbuf.at[me], kbuf.at[me], qbuf.at[z])[kind]
        return pltpu.make_async_copy(src, dst, own_sem.at[0] if kind == 2 else kv_recv.at[kind, z])

    def arrival(kind, d):
        slot = column(d)
        buf = (vbuf, kbuf)[kind]
        return waiting(buf.at[half * Z + slot], kv_send.at[0], kv_recv.at[kind, slot])

    def order_piece(d):
        to = column(d)
        return pltpu.make_async_remote_copy(
            src_ref=order_hbm,
            dst_ref=ord_in.at[half, z],
            send_sem=ord_send.at[0],
            recv_sem=ord_recv.at[0],
            device_id={"seq": half * Z + to},
            device_id_type=MESH,
        )

    def own_order():
        return pltpu.make_async_copy(order_hbm, ord_in.at[half, z], own_sem.at[1])

    def forward(kind, slot, side):
        buf = (vbuf, kbuf)[kind]
        return pltpu.make_async_remote_copy(
            src_ref=buf.at[side * Z + slot],
            dst_ref=buf.at[side * Z + slot],
            send_sem=fwd_send.at[0],
            recv_sem=fwd_recv.at[0],
            device_id=partner,
            device_id_type=MESH,
        )

    def own_value():
        return pltpu.make_async_remote_copy(
            src_ref=v_hbm.at[mine],
            dst_ref=vbuf.at[me],
            send_sem=fwd_send.at[0],
            recv_sem=fwd_recv.at[0],
            device_id=partner,
            device_id_type=MESH,
        )

    all_forwards = waiting(kbuf, fwd_send.at[0], fwd_recv.at[0])

    def order_forward(side):
        return pltpu.make_async_remote_copy(
            src_ref=ord_in.at[side],
            dst_ref=ord_in.at[side],
            send_sem=ofw_send.at[0],
            recv_sem=ofw_recv.at[0],
            device_id=partner,
            device_id_type=MESH,
        )

    def to_all(make):
        for d in FAR_FIRST[:-1]:
            _, there = owner_of(column(d), shift, core)

            @pl.when(there)
            def _(d=d):
                make(d)

    to_all(lambda d: order_piece(d).start())
    to_all(lambda d: piece(0, d).start())

    @pl.when(busy)
    def _():
        own_value().start()
        own_order().start()
        own_piece(0).start()

    def squares(raw):
        total = jnp.zeros((ROWS, ROWS), F32)
        for j in range(STREAMS):
            x = raw[j].astype(F32)
            total = total + x * x
        return jnp.sum(total.T, axis=0, keepdims=True)

    sum_out[...] = jnp.zeros((8, ROWS), F32)
    q_in.wait()
    sum_out[pl.ds(0, 1), :] = squares(qraw)
    k_in.wait()
    sum_out[pl.ds(1, 1), :] = squares(kraw)
    for d in range(1, GROUP):
        sum_copy(d).start()
    for copy in small:
        copy.wait()
    total = sum_out[...]
    all_sums.wait_recv()
    for d in range(1, GROUP):
        total = total + sum_in[lax.rem(member + d, GROUP)]
    scale = lax.rsqrt(total * (1.0 / (HEADS * ROWS)) + EPS)

    def by_row(row):
        return jnp.broadcast_to(scale[row : row + 1, :], (ROWS, ROWS)).T

    def normalize(kind, d, rows):
        stream, _ = owner_of(column(d), shift, core)
        raw, gains, out = ((kraw, kg_ref, kn), (qraw, qg_ref, qn))[kind - 1]
        gain = gains[pl.ds(member * STREAMS + stream, 1), :]
        out[stream] = (raw[stream].astype(F32) * rows * gain).astype(BF16)

    rows = by_row(1)

    def ready_key(d):
        normalize(1, d, rows)
        piece(1, d).start()

    to_all(ready_key)

    @pl.when(busy)
    def _():
        normalize(1, 0, rows)
        own_piece(1).start()

    rows_q = by_row(0)

    @pl.when(jnp.logical_not(busy))
    def _():
        to_all(lambda d: normalize(2, d, rows_q))
        to_all(lambda d: piece(2, d).start())

    def result(slot):
        return pltpu.make_async_remote_copy(
            src_ref=obuf.at[slot],
            dst_ref=out_ref.at[mine],
            send_sem=out_send.at[0],
            recv_sem=out_recv.at[0],
            device_id={"seq": half * Z + slot},
            device_id_type=MESH,
        )

    def own_result():
        return pltpu.make_async_copy(obuf.at[z], out_ref.at[mine], own_sem.at[2])

    @pl.when(busy)
    def _():
        for d in FAR_FIRST[:V_FIRST]:
            arrival(0, d).wait_recv()
            forward(0, column(d), half).start()

        def ready_query(d):
            normalize(2, d, rows_q)
            piece(2, d).start()

        to_all(ready_query)
        normalize(2, 0, rows_q)
        own_piece(2).start()
        own_order().wait()
        waiting(ord_in.at[half, pl.ds(0, Z - 1)], ord_send.at[0], ord_recv.at[0]).wait_recv()
        order_forward(half).start()
        for d in FAR_FIRST[V_FIRST:-1]:
            arrival(0, d).wait_recv()
            forward(0, column(d), half).start()
        own_piece(0).wait()
        own_piece(1).wait()
        forward(1, z, half).start()
        for d in FAR_FIRST[:4]:
            arrival(1, d).wait_recv()
            forward(1, column(d), half).start()

        order_forward(1 - half).wait_recv()
        tokens = ord_in[:, :, pl.ds(mine, 1), :].reshape(CLUSTERS, ROWS)
        place = lax.broadcasted_iota(jnp.int32, (CLUSTERS, ROWS), 0) * ROWS
        place = place + lax.broadcasted_iota(jnp.int32, (CLUSTERS, ROWS), 1)
        owner = jnp.full((CLUSTERS, ROWS), -1, jnp.int32)
        start = jnp.zeros((CLUSTERS, ROWS), jnp.int32)
        at = jnp.int32(0)
        for o in range(CLUSTERS):
            begun = place >= at
            owner = owner + begun.astype(jnp.int32)
            start = jnp.where(begun, at, start)
            at = at + rows_ref[mine, o]
        block = (owner * 2 + jnp.right_shift(place - start, 7)).astype(F32)
        high = jnp.right_shift(tokens, 7)
        low = jnp.bitwise_and(tokens, ROWS - 1)
        digit = lax.broadcasted_iota(jnp.int32, (ROWS, ROWS), 0)
        digit_high = lax.broadcasted_iota(jnp.int32, (CLUSTERS, ROWS), 0)
        for i in range(CLUSTERS):
            span = pl.ds(i * ROWS, ROWS)
            hit = digit == jnp.broadcast_to(low[i : i + 1], (ROWS, ROWS))
            bt_scr[:, span] = jnp.where(hit, 1.0, 0.0).astype(BF16)
            hit = digit_high == jnp.broadcast_to(high[i : i + 1], (CLUSTERS, ROWS))
            here = jnp.broadcast_to(block[i : i + 1], (CLUSTERS, ROWS))
            a_scr[:, span] = jnp.where(hit, here, 0.0).astype(BF16)
        by_low = lax.dot_general(
            bt_scr[...], a_scr[...], (((1,), (1,)), ((), ())), preferred_element_type=F32
        ).astype(BF16)
        lane = lax.broadcasted_iota(jnp.int32, (CLUSTERS, ROWS * CLUSTERS), 1)
        spread = jnp.right_shift(lane, 7) == lax.broadcasted_iota(
            jnp.int32, (CLUSTERS, ROWS * CLUSTERS), 0
        )
        wide = jnp.dot(
            by_low, jnp.where(spread, 1.0, 0.0).astype(BF16), preferred_element_type=F32
        )
        which = lax.broadcasted_iota(jnp.int32, (ROWS, ROWS), 1).astype(F32)
        for i in range(CLUSTERS):
            hit = wide[:, i * ROWS : (i + 1) * ROWS] == which
            oht[i] = jnp.where(hit, 1.0, 0.0).astype(BF16)
        mbuf[...] = jnp.zeros((ROWS, ROWS), BF16)
        same = lax.broadcasted_iota(jnp.int32, (BLOCKS, BLOCKS), 0) == (
            lax.broadcasted_iota(jnp.int32, (BLOCKS, BLOCKS), 1)
        )
        open_ = jnp.logical_or(map_ref[mine] == 1, same)
        mbuf[pl.ds(0, BLOCKS), pl.ds(0, BLOCKS)] = jnp.where(open_, 0.0, MASKED).astype(BF16)

        for d in FAR_FIRST[4:-1]:
            arrival(1, d).wait_recv()
            forward(1, column(d), half).start()

        factor = math.log2(math.e) / math.sqrt(ROWS)

        def score(left, side, start, into):
            peak = start
            for i in range(PARTS):
                span = pl.ds(side * Z + i * PER, PER)
                keys = kbuf[span].reshape(KEY_CHUNK, ROWS)
                tags = oht[span].reshape(KEY_CHUNK, ROWS)
                scores = lax.dot_general(
                    left,
                    jnp.concatenate([keys, tags], axis=1),
                    (((1,), (1,)), ((), ())),
                    preferred_element_type=F32,
                )
                into[:, pl.ds(i * KEY_CHUNK, KEY_CHUNK)] = scores
                peak = jnp.maximum(peak, jnp.max(scores, axis=1, keepdims=True))
            return peak

        def mix(peak, side, held):
            denom = jnp.zeros((2 * ROWS, 1), F32)
            mixed = jnp.zeros((2 * ROWS, ROWS), F32)
            for i in range(PARTS):
                span = pl.ds(side * Z + i * PER, PER)
                p = jnp.exp2((held[:, pl.ds(i * KEY_CHUNK, KEY_CHUNK)] - peak) * factor)
                denom = denom + jnp.sum(p, axis=1, keepdims=True)
                values = vbuf[span].reshape(KEY_CHUNK, ROWS)
                mixed = mixed + jnp.dot(p.astype(BF16), values, preferred_element_type=F32)
            return denom, mixed

        def near_half(t, carry):
            first, second = 4 + t, 3 - t
            @pl.when(t < 3)
            def _():
                waiting(qbuf.at[pl.ds(0, 2)], kv_send.at[0], q_recv.at[t]).wait_recv()

            @pl.when(t == 3)
            def _():
                waiting(qbuf.at[0], kv_send.at[0], q_recv.at[t]).wait_recv()
                own_piece(2).wait()

            lefts = []
            for d in (first, second):
                slot = column(d)
                bias = jnp.dot(oht[half * Z + slot], mbuf[...], preferred_element_type=F32)
                left = jnp.concatenate([qbuf[slot], bias.astype(BF16)], axis=1)
                lbuf[slot] = left
                lefts.append(left)
            start = jnp.full((2 * ROWS, 1), -jnp.inf, F32)
            peak = score(jnp.concatenate(lefts, axis=0), half, start, s_scr)
            denom, mixed = mix(peak, half, s_scr)
            for i, d in enumerate((first, second)):
                slot = column(d)
                rows = slice(i * ROWS, (i + 1) * ROWS)
                peaks[slot] = peak[rows]
                denoms[slot] = denom[rows]
                mixes[slot] = mixed[rows]
            return carry

        lax.fori_loop(0, Z // 2, near_half, 0)
        all_forwards.wait_recv()

        def far_score(t):
            slots = (column(4 + t), column(3 - t))
            left = jnp.concatenate([lbuf[slot] for slot in slots], axis=0)
            before = jnp.concatenate([peaks[slot] for slot in slots], axis=0)
            return before, score(left, 1 - half, before, (s_scr, s_two)[t % 2])

        def far_mix(t, before, peak):
            slots = (column(4 + t), column(3 - t))
            denom, mixed = mix(peak, 1 - half, (s_scr, s_two)[t % 2])
            fade = jnp.exp2((before - peak) * factor)
            denom = denom + fade * jnp.concatenate([denoms[slot] for slot in slots], axis=0)
            mixed = mixed + fade * jnp.concatenate([mixes[slot] for slot in slots], axis=0)
            out = (mixed / denom).astype(BF16)
            for i, slot in enumerate(slots):
                obuf[slot] = out[i * ROWS : (i + 1) * ROWS]

        held = far_score(0)
        for t in range(Z // 2):
            ahead = far_score(t + 1) if t < 3 else None
            far_mix(t, *held)
            held = ahead
            result(column(4 + t)).start()
            if t < 3:
                result(column(3 - t)).start()
        own_result().start()

    all_sums.wait_send()
    @pl.when(busy)
    def _():
        order_forward(half).wait_send()
        all_forwards.wait_send()
        waiting(obuf.at[pl.ds(0, Z - 1)], out_send.at[0], out_recv.at[0]).wait_send()
        own_result().wait()

    def settle(streams):
        waiting(ord_in.at[0, pl.ds(0, streams)], ord_send.at[0], ord_recv.at[0]).wait_send()
        waiting(kbuf.at[pl.ds(0, 3 * streams)], kv_send.at[0], kv_recv.at[0, 0]).wait_send()
        waiting(obuf.at[pl.ds(0, streams)], out_send.at[0], out_recv.at[0]).wait_recv()

    @pl.when(busy)
    def _():
        settle(STREAMS - 1)

    @pl.when(jnp.logical_not(busy))
    def _():
        settle(STREAMS)


def local(query, key, value, q_gain, k_gain, order, cluster_rows, block_map):
    streams = query.shape[0]
    any_ = pl.BlockSpec(memory_space=pl.ANY)
    sems = pltpu.SemaphoreType.DMA
    return pl.pallas_call(
        kernel,
        out_shape=pltpu.VMEM((streams, ROWS, ROWS), BF16),
        in_specs=[any_] * 8,
        out_specs=any_,
        scratch_shapes=[
            pltpu.VMEM((HEADS, ROWS), F32),
            pltpu.VMEM((HEADS, ROWS), F32),
            pltpu.SMEM((STREAMS, CLUSTERS), jnp.int32),
            pltpu.VMEM((STREAMS, BLOCKS, BLOCKS), jnp.int32),
            pltpu.VMEM((STREAMS, ROWS, ROWS), BF16),
            pltpu.VMEM((STREAMS, ROWS, ROWS), BF16),
            pltpu.VMEM((STREAMS, ROWS, ROWS), BF16),
            pltpu.VMEM((STREAMS, ROWS, ROWS), BF16),
            pltpu.VMEM((8, ROWS), F32),
            pltpu.VMEM((GROUP, 8, ROWS), F32),
            pltpu.VMEM((2, Z, STREAMS, ROWS), jnp.int32),
            pltpu.VMEM((2 * Z, ROWS, ROWS), BF16),
            pltpu.VMEM((2 * Z, ROWS, ROWS), BF16),
            pltpu.VMEM((Z, ROWS, ROWS), BF16),
            pltpu.VMEM((Z, ROWS, ROWS), BF16),
            pltpu.VMEM((2 * Z, ROWS, ROWS), BF16),
            pltpu.VMEM((ROWS, ROWS), BF16),
            pltpu.VMEM((Z, ROWS, 2 * ROWS), BF16),
            pltpu.VMEM((Z, ROWS, 1), F32),
            pltpu.VMEM((Z, ROWS, 1), F32),
            pltpu.VMEM((Z, ROWS, ROWS), F32),
            pltpu.VMEM((2 * ROWS, Z * ROWS), F32),
            pltpu.VMEM((2 * ROWS, Z * ROWS), F32),
            pltpu.VMEM((ROWS, 2 * Z * ROWS), BF16),
            pltpu.VMEM((CLUSTERS, 2 * Z * ROWS), BF16),
            sems((6,)),
            sems((3,)),
            sems((1,)),
            sems((1,)),
            sems((1,)),
            sems((1,)),
            sems((1,)),
            sems((2, Z)),
            sems((4,)),
            sems((1,)),
            sems((1,)),
            sems((1,)),
            sems((1,)),
            sems((1,)),
            sems((1,)),
        ],
        compiler_params=pltpu.CompilerParams(collective_id=0, has_side_effects=True),
        name="attend",
    )(query, key, value, q_gain, k_gain, order, cluster_rows, block_map)


def solution(mesh):
    return jax.shard_map(
        local,
        mesh=mesh,
        in_specs=(
            P("head", "seq", None),
            P("head", "seq", None),
            P("head", "seq", None),
            P(),
            P(),
            P("head", "seq"),
            P("head", None),
            P("head", None, None),
        ),
        out_specs=P("head", "seq", None),
        check_vma=False,
    )
```

```python
import math

import jax
import jax.numpy as jnp
from jax import lax
from jax.experimental import pallas as pl
from jax.experimental.pallas import tpu as pltpu
from jax.sharding import PartitionSpec as P

MESH = pl.DeviceIdType.MESH
F32 = jnp.float32
BF16 = jnp.bfloat16

EPS = 1e-06
ROWS = 128
Z = 8
STREAMS = 5
HEADS = 40
GROUP = 8
CLUSTERS = 16
BLOCKS = 32
MASKED = -(2.0**30)
FAR_FIRST = (4, 3, 5, 2, 6, 1, 7, 0)
KEY_CHUNK = 512
V_FIRST = 2
PER = KEY_CHUNK // ROWS
PARTS = Z // PER


def owner_of(z, shift, core):
    v = lax.rem(z - shift + 3 * core + 16, Z)
    stream = jnp.minimum(v - 3 * core * (v // 7), STREAMS - 1)
    busy = jnp.logical_or(v < STREAMS - core, core * v == 7)
    return stream, busy


def pair_of(d):
    return d - 4 if d >= 4 else 3 - d


def kernel(
    q_hbm, k_hbm, v_hbm, qg_hbm, kg_hbm, order_hbm, rows_hbm, map_hbm, out_ref,
    qg_ref, kg_ref, rows_ref, map_ref, qraw, kraw, qn, kn, sum_out, sum_in, ord_in, kbuf, vbuf, qbuf, obuf,
    oht, mbuf, lbuf, peaks, denoms, mixes, s_scr, s_two, bt_scr, a_scr,
    raw_sem, own_sem, sum_send, sum_recv, ord_send, ord_recv, kv_send, kv_recv, q_recv, fwd_send, fwd_recv,
    ofw_send, ofw_recv, out_send, out_recv,
):
    me = lax.axis_index("seq")
    head = lax.axis_index("head")
    half, z = me // Z, lax.rem(me, Z)
    shift = 2 * lax.rem(head // 2, 2)
    core = lax.rem(head, 2)
    member = lax.rem(head, GROUP)
    video = head - member
    mine, busy = owner_of(z, shift, core)
    partner = {"seq": (1 - half) * Z + z}

    def column(d):
        return lax.rem(z + d, Z)

    barrier = pltpu.get_barrier_semaphore()
    for d in range(1, Z):
        pl.semaphore_signal(
            barrier, inc=1, device_id={"seq": half * Z + column(d)}, device_id_type=MESH
        )
        pl.semaphore_signal(
            barrier,
            inc=1,
            device_id={"head": video + lax.rem(member + d, GROUP)},
            device_id_type=MESH,
        )
    pl.semaphore_signal(barrier, inc=1, device_id=partner, device_id_type=MESH)

    q_in = pltpu.make_async_copy(q_hbm, qraw, raw_sem.at[0])
    k_in = pltpu.make_async_copy(k_hbm, kraw, raw_sem.at[1])
    small = [
        pltpu.make_async_copy(src, dst, raw_sem.at[2 + i])
        for i, (src, dst) in enumerate(
            (
                (kg_hbm, kg_ref),
                (qg_hbm, qg_ref),
                (rows_hbm, rows_ref),
                (map_hbm, map_ref),
            )
        )
    ]
    q_in.start()
    k_in.start()
    for copy in small:
        copy.start()
    pl.semaphore_wait(barrier, 2 * (Z - 1) + 1)

    def sum_copy(d):
        return pltpu.make_async_remote_copy(
            src_ref=sum_out,
            dst_ref=sum_in.at[member],
            send_sem=sum_send.at[0],
            recv_sem=sum_recv.at[0],
            device_id={"head": video + lax.rem(member + d, GROUP)},
            device_id_type=MESH,
        )

    def waiting(ref, send_sem, recv_sem):
        return pltpu.make_async_remote_copy(
            src_ref=ref,
            dst_ref=ref,
            send_sem=send_sem,
            recv_sem=recv_sem,
            device_id=partner,
            device_id_type=MESH,
        )

    all_sums = waiting(sum_in.at[pl.ds(0, GROUP - 1)], sum_send.at[0], sum_recv.at[0])

    def piece(kind, d):
        to = column(d)
        stream, _ = owner_of(to, shift, core)
        src = (v_hbm, kn, qn)[kind].at[stream]
        dst = (vbuf.at[me], kbuf.at[me], qbuf.at[z])[kind]
        return pltpu.make_async_remote_copy(
            src_ref=src,
            dst_ref=dst,
            send_sem=kv_send.at[0],
            recv_sem=q_recv.at[pair_of(Z - d)] if kind == 2 else kv_recv.at[kind, z],
            device_id={"seq": half * Z + to},
            device_id_type=MESH,
        )

    def own_piece(kind):
        src = (v_hbm, kn, qn)[kind].at[mine]
        dst = (vbuf.at[me], kbuf.at[me], qbuf.at[z])[kind]
        return pltpu.make_async_copy(src, dst, own_sem.at[0] if kind == 2 else kv_recv.at[kind, z])

    def arrival(kind, d):
        slot = column(d)
        buf = (vbuf, kbuf)[kind]
        return waiting(buf.at[half * Z + slot], kv_send.at[0], kv_recv.at[kind, slot])

    def order_piece(d):
        to = column(d)
        return pltpu.make_async_remote_copy(
            src_ref=order_hbm,
            dst_ref=ord_in.at[half, z],
            send_sem=ord_send.at[0],
            recv_sem=ord_recv.at[0],
            device_id={"seq": half * Z + to},
            device_id_type=MESH,
        )

    def own_order():
        return pltpu.make_async_copy(order_hbm, ord_in.at[half, z], own_sem.at[1])

    def forward(kind, slot, side):
        buf = (vbuf, kbuf)[kind]
        return pltpu.make_async_remote_copy(
            src_ref=buf.at[side * Z + slot],
            dst_ref=buf.at[side * Z + slot],
            send_sem=fwd_send.at[0],
            recv_sem=fwd_recv.at[0],
            device_id=partner,
            device_id_type=MESH,
        )

    def own_key():
        return pltpu.make_async_remote_copy(
            src_ref=kn.at[mine],
            dst_ref=kbuf.at[me],
            send_sem=fwd_send.at[0],
            recv_sem=fwd_recv.at[0],
            device_id=partner,
            device_id_type=MESH,
        )

    def own_value():
        return pltpu.make_async_remote_copy(
            src_ref=v_hbm.at[mine],
            dst_ref=vbuf.at[me],
            send_sem=fwd_send.at[0],
            recv_sem=fwd_recv.at[0],
            device_id=partner,
            device_id_type=MESH,
        )

    all_forwards = waiting(kbuf, fwd_send.at[0], fwd_recv.at[0])

    def order_forward(side):
        return pltpu.make_async_remote_copy(
            src_ref=ord_in.at[side],
            dst_ref=ord_in.at[side],
            send_sem=ofw_send.at[0],
            recv_sem=ofw_recv.at[0],
            device_id=partner,
            device_id_type=MESH,
        )

    def to_all(make):
        for d in FAR_FIRST[:-1]:
            _, there = owner_of(column(d), shift, core)

            @pl.when(there)
            def _(d=d):
                make(d)

    to_all(lambda d: order_piece(d).start())
    to_all(lambda d: piece(0, d).start())

    @pl.when(busy)
    def _():
        own_value().start()
        own_order().start()
        own_piece(0).start()

    def squares(raw):
        total = jnp.zeros((ROWS, ROWS), F32)
        for j in range(STREAMS):
            x = raw[j].astype(F32)
            total = total + x * x
        return jnp.sum(total.T, axis=0, keepdims=True)

    sum_out[...] = jnp.zeros((8, ROWS), F32)
    q_in.wait()
    sum_out[pl.ds(0, 1), :] = squares(qraw)
    k_in.wait()
    sum_out[pl.ds(1, 1), :] = squares(kraw)
    for d in range(1, GROUP):
        sum_copy(d).start()
    for copy in small:
        copy.wait()
    total = sum_out[...]
    all_sums.wait_recv()
    for d in range(1, GROUP):
        total = total + sum_in[lax.rem(member + d, GROUP)]
    scale = lax.rsqrt(total * (1.0 / (HEADS * ROWS)) + EPS)

    def by_row(row):
        return jnp.broadcast_to(scale[row : row + 1, :], (ROWS, ROWS)).T

    def normalize(kind, d, rows):
        stream, _ = owner_of(column(d), shift, core)
        raw, gains, out = ((kraw, kg_ref, kn), (qraw, qg_ref, qn))[kind - 1]
        gain = gains[pl.ds(member * STREAMS + stream, 1), :]
        out[stream] = (raw[stream].astype(F32) * rows * gain).astype(BF16)

    rows = by_row(1)

    def ready_key(d):
        normalize(1, d, rows)
        piece(1, d).start()

    to_all(ready_key)

    @pl.when(busy)
    def _():
        normalize(1, 0, rows)
        own_piece(1).start()
        own_key().start()

    rows_q = by_row(0)

    @pl.when(jnp.logical_not(busy))
    def _():
        to_all(lambda d: normalize(2, d, rows_q))
        to_all(lambda d: piece(2, d).start())

    def result(slot):
        return pltpu.make_async_remote_copy(
            src_ref=obuf.at[slot],
            dst_ref=out_ref.at[mine],
            send_sem=out_send.at[0],
            recv_sem=out_recv.at[0],
            device_id={"seq": half * Z + slot},
            device_id_type=MESH,
        )

    def own_result():
        return pltpu.make_async_copy(obuf.at[z], out_ref.at[mine], own_sem.at[2])

    @pl.when(busy)
    def _():
        for d in FAR_FIRST[:V_FIRST]:
            arrival(0, d).wait_recv()
            forward(0, column(d), half).start()

        def ready_query(d):
            normalize(2, d, rows_q)
            piece(2, d).start()

        to_all(ready_query)
        normalize(2, 0, rows_q)
        own_piece(2).start()
        own_order().wait()
        waiting(ord_in.at[half, pl.ds(0, Z - 1)], ord_send.at[0], ord_recv.at[0]).wait_recv()
        order_forward(half).start()
        for d in FAR_FIRST[V_FIRST:-1]:
            arrival(0, d).wait_recv()
            forward(0, column(d), half).start()
        own_piece(0).wait()
        order_forward(1 - half).wait_recv()
        tokens = ord_in[:, :, pl.ds(mine, 1), :].reshape(CLUSTERS, ROWS)
        place = lax.broadcasted_iota(jnp.int32, (CLUSTERS, ROWS), 0) * ROWS
        place = place + lax.broadcasted_iota(jnp.int32, (CLUSTERS, ROWS), 1)
        owner = jnp.full((CLUSTERS, ROWS), -1, jnp.int32)
        start = jnp.zeros((CLUSTERS, ROWS), jnp.int32)
        at = jnp.int32(0)
        for o in range(CLUSTERS):
            begun = place >= at
            owner = owner + begun.astype(jnp.int32)
            start = jnp.where(begun, at, start)
            at = at + rows_ref[mine, o]
        block = (owner * 2 + jnp.right_shift(place - start, 7)).astype(F32)
        high = jnp.right_shift(tokens, 7)
        low = jnp.bitwise_and(tokens, ROWS - 1)
        digit = lax.broadcasted_iota(jnp.int32, (ROWS, ROWS), 0)
        digit_high = lax.broadcasted_iota(jnp.int32, (CLUSTERS, ROWS), 0)
        for i in range(CLUSTERS):
            span = pl.ds(i * ROWS, ROWS)
            hit = digit == jnp.broadcast_to(low[i : i + 1], (ROWS, ROWS))
            bt_scr[:, span] = jnp.where(hit, 1.0, 0.0).astype(BF16)
            hit = digit_high == jnp.broadcast_to(high[i : i + 1], (CLUSTERS, ROWS))
            here = jnp.broadcast_to(block[i : i + 1], (CLUSTERS, ROWS))
            a_scr[:, span] = jnp.where(hit, here, 0.0).astype(BF16)
        by_low = lax.dot_general(
            bt_scr[...], a_scr[...], (((1,), (1,)), ((), ())), preferred_element_type=F32
        ).astype(BF16)
        lane = lax.broadcasted_iota(jnp.int32, (CLUSTERS, ROWS * CLUSTERS), 1)
        spread = jnp.right_shift(lane, 7) == lax.broadcasted_iota(
            jnp.int32, (CLUSTERS, ROWS * CLUSTERS), 0
        )
        wide = jnp.dot(
            by_low, jnp.where(spread, 1.0, 0.0).astype(BF16), preferred_element_type=F32
        )
        which = lax.broadcasted_iota(jnp.int32, (ROWS, ROWS), 1).astype(F32)
        for i in range(CLUSTERS):
            hit = wide[:, i * ROWS : (i + 1) * ROWS] == which
            oht[i] = jnp.where(hit, 1.0, 0.0).astype(BF16)
        mbuf[...] = jnp.zeros((ROWS, ROWS), BF16)
        same = lax.broadcasted_iota(jnp.int32, (BLOCKS, BLOCKS), 0) == (
            lax.broadcasted_iota(jnp.int32, (BLOCKS, BLOCKS), 1)
        )
        open_ = jnp.logical_or(map_ref[mine] == 1, same)
        mbuf[pl.ds(0, BLOCKS), pl.ds(0, BLOCKS)] = jnp.where(open_, 0.0, MASKED).astype(BF16)

        own_piece(1).wait()
        for d in FAR_FIRST[:4]:
            arrival(1, d).wait_recv()
            forward(1, column(d), half).start()
        for d in FAR_FIRST[4:-1]:
            arrival(1, d).wait_recv()
            forward(1, column(d), half).start()

        factor = math.log2(math.e) / math.sqrt(ROWS)

        def score(left, side, start, into):
            peak = start
            for i in range(PARTS):
                span = pl.ds(side * Z + i * PER, PER)
                keys = kbuf[span].reshape(KEY_CHUNK, ROWS)
                tags = oht[span].reshape(KEY_CHUNK, ROWS)
                scores = lax.dot_general(
                    left,
                    jnp.concatenate([keys, tags], axis=1),
                    (((1,), (1,)), ((), ())),
                    preferred_element_type=F32,
                )
                into[:, pl.ds(i * KEY_CHUNK, KEY_CHUNK)] = scores
                peak = jnp.maximum(peak, jnp.max(scores, axis=1, keepdims=True))
            return peak

        def mix(peak, side, held):
            denom = jnp.zeros((2 * ROWS, 1), F32)
            mixed = jnp.zeros((2 * ROWS, ROWS), F32)
            for i in range(PARTS):
                span = pl.ds(side * Z + i * PER, PER)
                p = jnp.exp2((held[:, pl.ds(i * KEY_CHUNK, KEY_CHUNK)] - peak) * factor)
                denom = denom + jnp.sum(p, axis=1, keepdims=True)
                values = vbuf[span].reshape(KEY_CHUNK, ROWS)
                mixed = mixed + jnp.dot(p.astype(BF16), values, preferred_element_type=F32)
            return denom, mixed

        def near_half(t, carry):
            first, second = 4 + t, 3 - t
            @pl.when(t < 3)
            def _():
                waiting(qbuf.at[pl.ds(0, 2)], kv_send.at[0], q_recv.at[t]).wait_recv()

            @pl.when(t == 3)
            def _():
                waiting(qbuf.at[0], kv_send.at[0], q_recv.at[t]).wait_recv()
                own_piece(2).wait()

            lefts = []
            for d in (first, second):
                slot = column(d)
                bias = jnp.dot(oht[half * Z + slot], mbuf[...], preferred_element_type=F32)
                left = jnp.concatenate([qbuf[slot], bias.astype(BF16)], axis=1)
                lbuf[slot] = left
                lefts.append(left)
            start = jnp.full((2 * ROWS, 1), -jnp.inf, F32)
            peak = score(jnp.concatenate(lefts, axis=0), half, start, s_scr)
            denom, mixed = mix(peak, half, s_scr)
            for i, d in enumerate((first, second)):
                slot = column(d)
                rows = slice(i * ROWS, (i + 1) * ROWS)
                peaks[slot] = peak[rows]
                denoms[slot] = denom[rows]
                mixes[slot] = mixed[rows]
            return carry

        lax.fori_loop(0, Z // 2, near_half, 0)
        all_forwards.wait_recv()

        def far_score(t):
            slots = (column(4 + t), column(3 - t))
            left = jnp.concatenate([lbuf[slot] for slot in slots], axis=0)
            before = jnp.concatenate([peaks[slot] for slot in slots], axis=0)
            return before, score(left, 1 - half, before, (s_scr, s_two)[t % 2])

        def far_mix(t, before, peak):
            slots = (column(4 + t), column(3 - t))
            denom, mixed = mix(peak, 1 - half, (s_scr, s_two)[t % 2])
            fade = jnp.exp2((before - peak) * factor)
            denom = denom + fade * jnp.concatenate([denoms[slot] for slot in slots], axis=0)
            mixed = mixed + fade * jnp.concatenate([mixes[slot] for slot in slots], axis=0)
            out = (mixed / denom).astype(BF16)
            for i, slot in enumerate(slots):
                obuf[slot] = out[i * ROWS : (i + 1) * ROWS]

        held = far_score(0)
        for t in range(Z // 2):
            ahead = far_score(t + 1) if t < 3 else None
            far_mix(t, *held)
            held = ahead
            result(column(4 + t)).start()
            if t < 3:
                result(column(3 - t)).start()
        own_result().start()

    all_sums.wait_send()
    @pl.when(busy)
    def _():
        order_forward(half).wait_send()
        all_forwards.wait_send()
        waiting(obuf.at[pl.ds(0, Z - 1)], out_send.at[0], out_recv.at[0]).wait_send()
        own_result().wait()

    def settle(streams):
        waiting(ord_in.at[0, pl.ds(0, streams)], ord_send.at[0], ord_recv.at[0]).wait_send()
        waiting(kbuf.at[pl.ds(0, 3 * streams)], kv_send.at[0], kv_recv.at[0, 0]).wait_send()
        waiting(obuf.at[pl.ds(0, streams)], out_send.at[0], out_recv.at[0]).wait_recv()

    @pl.when(busy)
    def _():
        settle(STREAMS - 1)

    @pl.when(jnp.logical_not(busy))
    def _():
        settle(STREAMS)


def local(query, key, value, q_gain, k_gain, order, cluster_rows, block_map):
    streams = query.shape[0]
    any_ = pl.BlockSpec(memory_space=pl.ANY)
    sems = pltpu.SemaphoreType.DMA
    return pl.pallas_call(
        kernel,
        out_shape=pltpu.VMEM((streams, ROWS, ROWS), BF16),
        in_specs=[any_] * 8,
        out_specs=any_,
        scratch_shapes=[
            pltpu.VMEM((HEADS, ROWS), F32),
            pltpu.VMEM((HEADS, ROWS), F32),
            pltpu.SMEM((STREAMS, CLUSTERS), jnp.int32),
            pltpu.VMEM((STREAMS, BLOCKS, BLOCKS), jnp.int32),
            pltpu.VMEM((STREAMS, ROWS, ROWS), BF16),
            pltpu.VMEM((STREAMS, ROWS, ROWS), BF16),
            pltpu.VMEM((STREAMS, ROWS, ROWS), BF16),
            pltpu.VMEM((STREAMS, ROWS, ROWS), BF16),
            pltpu.VMEM((8, ROWS), F32),
            pltpu.VMEM((GROUP, 8, ROWS), F32),
            pltpu.VMEM((2, Z, STREAMS, ROWS), jnp.int32),
            pltpu.VMEM((2 * Z, ROWS, ROWS), BF16),
            pltpu.VMEM((2 * Z, ROWS, ROWS), BF16),
            pltpu.VMEM((Z, ROWS, ROWS), BF16),
            pltpu.VMEM((Z, ROWS, ROWS), BF16),
            pltpu.VMEM((2 * Z, ROWS, ROWS), BF16),
            pltpu.VMEM((ROWS, ROWS), BF16),
            pltpu.VMEM((Z, ROWS, 2 * ROWS), BF16),
            pltpu.VMEM((Z, ROWS, 1), F32),
            pltpu.VMEM((Z, ROWS, 1), F32),
            pltpu.VMEM((Z, ROWS, ROWS), F32),
            pltpu.VMEM((2 * ROWS, Z * ROWS), F32),
            pltpu.VMEM((2 * ROWS, Z * ROWS), F32),
            pltpu.VMEM((ROWS, 2 * Z * ROWS), BF16),
            pltpu.VMEM((CLUSTERS, 2 * Z * ROWS), BF16),
            sems((6,)),
            sems((3,)),
            sems((1,)),
            sems((1,)),
            sems((1,)),
            sems((1,)),
            sems((1,)),
            sems((2, Z)),
            sems((4,)),
            sems((1,)),
            sems((1,)),
            sems((1,)),
            sems((1,)),
            sems((1,)),
            sems((1,)),
        ],
        compiler_params=pltpu.CompilerParams(collective_id=0, has_side_effects=True),
        name="attend",
    )(query, key, value, q_gain, k_gain, order, cluster_rows, block_map)


def solution(mesh):
    return jax.shard_map(
        local,
        mesh=mesh,
        in_specs=(
            P("head", "seq", None),
            P("head", "seq", None),
            P("head", "seq", None),
            P(),
            P(),
            P("head", "seq"),
            P("head", None),
            P("head", None, None),
        ),
        out_specs=P("head", "seq", None),
        check_vma=False,
    )
```

```python
import math

import jax
import jax.numpy as jnp
from jax import lax
from jax.experimental import pallas as pl
from jax.experimental.pallas import tpu as pltpu
from jax.sharding import PartitionSpec as P

MESH = pl.DeviceIdType.MESH
F32 = jnp.float32
BF16 = jnp.bfloat16

EPS = 1e-06
ROWS = 128
Z = 8
STREAMS = 5
HEADS = 40
GROUP = 8
CLUSTERS = 16
BLOCKS = 32
MASKED = -(2.0**30)
FAR_FIRST = (4, 3, 5, 2, 6, 1, 7, 0)
KEY_CHUNK = 512
V_FIRST = 2
PER = KEY_CHUNK // ROWS
PARTS = Z // PER


def owner_of(z, shift, core):
    v = lax.rem(z - shift + 3 * core + 16, Z)
    stream = jnp.minimum(v - 3 * core * (v // 7), STREAMS - 1)
    busy = jnp.logical_or(v < STREAMS - core, core * v == 7)
    return stream, busy


def pair_of(d):
    return d - 4 if d >= 4 else 3 - d


def kernel(
    q_hbm, k_hbm, v_hbm, qg_hbm, kg_hbm, order_hbm, rows_hbm, map_hbm, out_ref,
    qg_ref, kg_ref, rows_ref, map_ref, qraw, kraw, qn, kn, sum_out, sum_in, ord_in, kbuf, vbuf, qbuf, obuf,
    oht, mbuf, lbuf, peaks, denoms, mixes, s_scr, s_two, bt_scr, a_scr,
    raw_sem, own_sem, sum_send, sum_recv, ord_send, ord_recv, kv_send, kv_recv, q_recv, fwd_send, fwd_recv,
    ofw_send, ofw_recv, out_send, out_recv,
):
    me = lax.axis_index("seq")
    head = lax.axis_index("head")
    half, z = me // Z, lax.rem(me, Z)
    shift = 2 * lax.rem(head // 2, 2)
    core = lax.rem(head, 2)
    member = lax.rem(head, GROUP)
    video = head - member
    mine, busy = owner_of(z, shift, core)
    partner = {"seq": (1 - half) * Z + z}

    def column(d):
        return lax.rem(z + d, Z)

    barrier = pltpu.get_barrier_semaphore()
    for d in range(1, Z):
        pl.semaphore_signal(
            barrier, inc=1, device_id={"seq": half * Z + column(d)}, device_id_type=MESH
        )
        pl.semaphore_signal(
            barrier,
            inc=1,
            device_id={"head": video + lax.rem(member + d, GROUP)},
            device_id_type=MESH,
        )
    pl.semaphore_signal(barrier, inc=1, device_id=partner, device_id_type=MESH)

    q_in = pltpu.make_async_copy(q_hbm, qraw, raw_sem.at[0])
    k_in = pltpu.make_async_copy(k_hbm, kraw, raw_sem.at[1])
    small = [
        pltpu.make_async_copy(src, dst, raw_sem.at[2 + i])
        for i, (src, dst) in enumerate(
            (
                (kg_hbm, kg_ref),
                (qg_hbm, qg_ref),
                (rows_hbm, rows_ref),
                (map_hbm, map_ref),
            )
        )
    ]
    q_in.start()
    k_in.start()
    for copy in small:
        copy.start()
    pl.semaphore_wait(barrier, 2 * (Z - 1) + 1)

    def sum_copy(d):
        return pltpu.make_async_remote_copy(
            src_ref=sum_out,
            dst_ref=sum_in.at[member],
            send_sem=sum_send.at[0],
            recv_sem=sum_recv.at[0],
            device_id={"head": video + lax.rem(member + d, GROUP)},
            device_id_type=MESH,
        )

    def waiting(ref, send_sem, recv_sem):
        return pltpu.make_async_remote_copy(
            src_ref=ref,
            dst_ref=ref,
            send_sem=send_sem,
            recv_sem=recv_sem,
            device_id=partner,
            device_id_type=MESH,
        )

    all_sums = waiting(sum_in.at[pl.ds(0, GROUP - 1)], sum_send.at[0], sum_recv.at[0])

    def piece(kind, d):
        to = column(d)
        stream, _ = owner_of(to, shift, core)
        src = (v_hbm, kn, qn)[kind].at[stream]
        dst = (vbuf.at[me], kbuf.at[me], qbuf.at[z])[kind]
        return pltpu.make_async_remote_copy(
            src_ref=src,
            dst_ref=dst,
            send_sem=kv_send.at[0],
            recv_sem=q_recv.at[pair_of(Z - d)] if kind == 2 else kv_recv.at[kind, z],
            device_id={"seq": half * Z + to},
            device_id_type=MESH,
        )

    def own_piece(kind):
        src = (v_hbm, kn, qn)[kind].at[mine]
        dst = (vbuf.at[me], kbuf.at[me], qbuf.at[z])[kind]
        return pltpu.make_async_copy(src, dst, own_sem.at[0] if kind == 2 else kv_recv.at[kind, z])

    def arrival(kind, d):
        slot = column(d)
        buf = (vbuf, kbuf)[kind]
        return waiting(buf.at[half * Z + slot], kv_send.at[0], kv_recv.at[kind, slot])

    def order_piece(d):
        to = column(d)
        return pltpu.make_async_remote_copy(
            src_ref=order_hbm,
            dst_ref=ord_in.at[half, z],
            send_sem=ord_send.at[0],
            recv_sem=ord_recv.at[0],
            device_id={"seq": half * Z + to},
            device_id_type=MESH,
        )

    def own_order():
        return pltpu.make_async_copy(order_hbm, ord_in.at[half, z], own_sem.at[1])

    def forward(kind, slot, side):
        buf = (vbuf, kbuf)[kind]
        return pltpu.make_async_remote_copy(
            src_ref=buf.at[side * Z + slot],
            dst_ref=buf.at[side * Z + slot],
            send_sem=fwd_send.at[0],
            recv_sem=fwd_recv.at[0],
            device_id=partner,
            device_id_type=MESH,
        )

    def own_key():
        return pltpu.make_async_remote_copy(
            src_ref=kn.at[mine],
            dst_ref=kbuf.at[me],
            send_sem=fwd_send.at[0],
            recv_sem=fwd_recv.at[0],
            device_id=partner,
            device_id_type=MESH,
        )

    def own_value():
        return pltpu.make_async_remote_copy(
            src_ref=v_hbm.at[mine],
            dst_ref=vbuf.at[me],
            send_sem=fwd_send.at[0],
            recv_sem=fwd_recv.at[0],
            device_id=partner,
            device_id_type=MESH,
        )

    all_forwards = waiting(kbuf, fwd_send.at[0], fwd_recv.at[0])

    def order_forward(side):
        return pltpu.make_async_remote_copy(
            src_ref=ord_in.at[side],
            dst_ref=ord_in.at[side],
            send_sem=ofw_send.at[0],
            recv_sem=ofw_recv.at[0],
            device_id=partner,
            device_id_type=MESH,
        )

    def to_all(make):
        for d in FAR_FIRST[:-1]:
            _, there = owner_of(column(d), shift, core)

            @pl.when(there)
            def _(d=d):
                make(d)

    to_all(lambda d: order_piece(d).start())
    to_all(lambda d: piece(0, d).start())

    @pl.when(busy)
    def _():
        own_value().start()
        own_order().start()
        own_piece(0).start()

    def squares(raw):
        total = jnp.zeros((ROWS, ROWS), F32)
        for j in range(STREAMS):
            x = raw[j].astype(F32)
            total = total + x * x
        return jnp.sum(total.T, axis=0, keepdims=True)

    sum_out[...] = jnp.zeros((8, ROWS), F32)
    q_in.wait()
    sum_out[pl.ds(0, 1), :] = squares(qraw)
    k_in.wait()
    sum_out[pl.ds(1, 1), :] = squares(kraw)
    for d in range(1, GROUP):
        sum_copy(d).start()
    for copy in small:
        copy.wait()
    total = sum_out[...]
    all_sums.wait_recv()
    for d in range(1, GROUP):
        total = total + sum_in[lax.rem(member + d, GROUP)]
    scale = lax.rsqrt(total * (1.0 / (HEADS * ROWS)) + EPS)

    def by_row(row):
        return jnp.broadcast_to(scale[row : row + 1, :], (ROWS, ROWS)).T

    def normalize(kind, d, rows):
        stream, _ = owner_of(column(d), shift, core)
        raw, gains, out = ((kraw, kg_ref, kn), (qraw, qg_ref, qn))[kind - 1]
        gain = gains[pl.ds(member * STREAMS + stream, 1), :]
        out[stream] = (raw[stream].astype(F32) * rows * gain).astype(BF16)

    rows = by_row(1)

    def ready_key(d):
        normalize(1, d, rows)
        piece(1, d).start()

    to_all(ready_key)

    @pl.when(busy)
    def _():
        normalize(1, 0, rows)
        own_piece(1).start()
        own_key().start()

    rows_q = by_row(0)

    def ready_query(d):
        normalize(2, d, rows_q)
        piece(2, d).start()


    @pl.when(jnp.logical_not(busy))
    def _():
        to_all(ready_query)

    def result(slot):
        return pltpu.make_async_remote_copy(
            src_ref=obuf.at[slot],
            dst_ref=out_ref.at[mine],
            send_sem=out_send.at[0],
            recv_sem=out_recv.at[0],
            device_id={"seq": half * Z + slot},
            device_id_type=MESH,
        )

    def own_result():
        return pltpu.make_async_copy(obuf.at[z], out_ref.at[mine], own_sem.at[2])

    @pl.when(busy)
    def _():
        for d in FAR_FIRST[:V_FIRST]:
            arrival(0, d).wait_recv()
            forward(0, column(d), half).start()

        to_all(ready_query)
        normalize(2, 0, rows_q)
        own_piece(2).start()
        own_order().wait()
        waiting(ord_in.at[half, pl.ds(0, Z - 1)], ord_send.at[0], ord_recv.at[0]).wait_recv()
        order_forward(half).start()
        for d in FAR_FIRST[V_FIRST:-1]:
            arrival(0, d).wait_recv()
            forward(0, column(d), half).start()
        own_piece(0).wait()
        order_forward(1 - half).wait_recv()
        tokens = ord_in[:, :, pl.ds(mine, 1), :].reshape(CLUSTERS, ROWS)
        place = lax.broadcasted_iota(jnp.int32, (CLUSTERS, ROWS), 0) * ROWS
        place = place + lax.broadcasted_iota(jnp.int32, (CLUSTERS, ROWS), 1)
        owner = jnp.full((CLUSTERS, ROWS), -1, jnp.int32)
        start = jnp.zeros((CLUSTERS, ROWS), jnp.int32)
        at = jnp.int32(0)
        for o in range(CLUSTERS):
            begun = place >= at
            owner = owner + begun.astype(jnp.int32)
            start = jnp.where(begun, at, start)
            at = at + rows_ref[mine, o]
        block = (owner * 2 + jnp.right_shift(place - start, 7)).astype(F32)
        high = jnp.right_shift(tokens, 7)
        low = jnp.bitwise_and(tokens, ROWS - 1)
        digit = lax.broadcasted_iota(jnp.int32, (ROWS, ROWS), 0)
        digit_high = lax.broadcasted_iota(jnp.int32, (CLUSTERS, ROWS), 0)
        for i in range(CLUSTERS):
            span = pl.ds(i * ROWS, ROWS)
            hit = digit == jnp.broadcast_to(low[i : i + 1], (ROWS, ROWS))
            bt_scr[:, span] = jnp.where(hit, 1.0, 0.0).astype(BF16)
            hit = digit_high == jnp.broadcast_to(high[i : i + 1], (CLUSTERS, ROWS))
            here = jnp.broadcast_to(block[i : i + 1], (CLUSTERS, ROWS))
            a_scr[:, span] = jnp.where(hit, here, 0.0).astype(BF16)
        by_low = lax.dot_general(
            bt_scr[...], a_scr[...], (((1,), (1,)), ((), ())), preferred_element_type=F32
        ).astype(BF16)
        lane = lax.broadcasted_iota(jnp.int32, (CLUSTERS, ROWS * CLUSTERS), 1)
        spread = jnp.right_shift(lane, 7) == lax.broadcasted_iota(
            jnp.int32, (CLUSTERS, ROWS * CLUSTERS), 0
        )
        wide = jnp.dot(
            by_low, jnp.where(spread, 1.0, 0.0).astype(BF16), preferred_element_type=F32
        )
        which = lax.broadcasted_iota(jnp.int32, (ROWS, ROWS), 1).astype(F32)
        for i in range(CLUSTERS):
            hit = wide[:, i * ROWS : (i + 1) * ROWS] == which
            oht[i] = jnp.where(hit, 1.0, 0.0).astype(BF16)
        mbuf[...] = jnp.zeros((ROWS, ROWS), BF16)
        same = lax.broadcasted_iota(jnp.int32, (BLOCKS, BLOCKS), 0) == (
            lax.broadcasted_iota(jnp.int32, (BLOCKS, BLOCKS), 1)
        )
        open_ = jnp.logical_or(map_ref[mine] == 1, same)
        mbuf[pl.ds(0, BLOCKS), pl.ds(0, BLOCKS)] = jnp.where(open_, 0.0, MASKED).astype(BF16)

        own_piece(1).wait()
        for d in FAR_FIRST[:4]:
            arrival(1, d).wait_recv()
            forward(1, column(d), half).start()
        for d in FAR_FIRST[4:-1]:
            arrival(1, d).wait_recv()
            forward(1, column(d), half).start()

        factor = math.log2(math.e) / math.sqrt(ROWS)

        def score(left, side, start, into):
            peak = start
            for i in range(PARTS):
                span = pl.ds(side * Z + i * PER, PER)
                keys = kbuf[span].reshape(KEY_CHUNK, ROWS)
                tags = oht[span].reshape(KEY_CHUNK, ROWS)
                scores = lax.dot_general(
                    left,
                    jnp.concatenate([keys, tags], axis=1),
                    (((1,), (1,)), ((), ())),
                    preferred_element_type=F32,
                )
                into[:, pl.ds(i * KEY_CHUNK, KEY_CHUNK)] = scores
                peak = jnp.maximum(peak, jnp.max(scores, axis=1, keepdims=True))
            return peak

        def mix(peak, side, held):
            denom = jnp.zeros((2 * ROWS, 1), F32)
            mixed = jnp.zeros((2 * ROWS, ROWS), F32)
            for i in range(PARTS):
                span = pl.ds(side * Z + i * PER, PER)
                p = jnp.exp2((held[:, pl.ds(i * KEY_CHUNK, KEY_CHUNK)] - peak) * factor)
                denom = denom + jnp.sum(p, axis=1, keepdims=True)
                values = vbuf[span].reshape(KEY_CHUNK, ROWS)
                mixed = mixed + jnp.dot(p.astype(BF16), values, preferred_element_type=F32)
            return denom, mixed

        def near_half(t, carry):
            first, second = 4 + t, 3 - t
            @pl.when(t < 3)
            def _():
                waiting(qbuf.at[pl.ds(0, 2)], kv_send.at[0], q_recv.at[t]).wait_recv()

            @pl.when(t == 3)
            def _():
                waiting(qbuf.at[0], kv_send.at[0], q_recv.at[t]).wait_recv()
                own_piece(2).wait()

            lefts = []
            for d in (first, second):
                slot = column(d)
                bias = jnp.dot(oht[half * Z + slot], mbuf[...], preferred_element_type=F32)
                left = jnp.concatenate([qbuf[slot], bias.astype(BF16)], axis=1)
                lbuf[slot] = left
                lefts.append(left)
            start = jnp.full((2 * ROWS, 1), -jnp.inf, F32)
            peak = score(jnp.concatenate(lefts, axis=0), half, start, s_scr)
            denom, mixed = mix(peak, half, s_scr)
            for i, d in enumerate((first, second)):
                slot = column(d)
                rows = slice(i * ROWS, (i + 1) * ROWS)
                peaks[slot] = peak[rows]
                denoms[slot] = denom[rows]
                mixes[slot] = mixed[rows]
            return carry

        lax.fori_loop(0, Z // 2, near_half, 0)
        all_forwards.wait_recv()

        def far_score(t):
            slots = (column(4 + t), column(3 - t))
            left = jnp.concatenate([lbuf[slot] for slot in slots], axis=0)
            before = jnp.concatenate([peaks[slot] for slot in slots], axis=0)
            return before, score(left, 1 - half, before, (s_scr, s_two)[t % 2])

        def far_mix(t, before, peak):
            slots = (column(4 + t), column(3 - t))
            denom, mixed = mix(peak, 1 - half, (s_scr, s_two)[t % 2])
            fade = jnp.exp2((before - peak) * factor)
            denom = denom + fade * jnp.concatenate([denoms[slot] for slot in slots], axis=0)
            mixed = mixed + fade * jnp.concatenate([mixes[slot] for slot in slots], axis=0)
            out = (mixed / denom).astype(BF16)
            for i, slot in enumerate(slots):
                obuf[slot] = out[i * ROWS : (i + 1) * ROWS]

        held = far_score(0)
        for t in range(Z // 2):
            ahead = far_score(t + 1) if t < 3 else None
            far_mix(t, *held)
            held = ahead
            result(column(4 + t)).start()
            if t < 3:
                result(column(3 - t)).start()
        own_result().start()

    all_sums.wait_send()
    @pl.when(busy)
    def _():
        order_forward(half).wait_send()
        all_forwards.wait_send()
        waiting(obuf.at[pl.ds(0, Z - 1)], out_send.at[0], out_recv.at[0]).wait_send()
        own_result().wait()

    def settle(streams):
        waiting(ord_in.at[0, pl.ds(0, streams)], ord_send.at[0], ord_recv.at[0]).wait_send()
        waiting(kbuf.at[pl.ds(0, 3 * streams)], kv_send.at[0], kv_recv.at[0, 0]).wait_send()
        waiting(obuf.at[pl.ds(0, streams)], out_send.at[0], out_recv.at[0]).wait_recv()

    @pl.when(busy)
    def _():
        settle(STREAMS - 1)

    @pl.when(jnp.logical_not(busy))
    def _():
        settle(STREAMS)


def local(query, key, value, q_gain, k_gain, order, cluster_rows, block_map):
    streams = query.shape[0]
    any_ = pl.BlockSpec(memory_space=pl.ANY)
    sems = pltpu.SemaphoreType.DMA
    return pl.pallas_call(
        kernel,
        out_shape=pltpu.VMEM((streams, ROWS, ROWS), BF16),
        in_specs=[any_] * 8,
        out_specs=any_,
        scratch_shapes=[
            pltpu.VMEM((HEADS, ROWS), F32),
            pltpu.VMEM((HEADS, ROWS), F32),
            pltpu.SMEM((STREAMS, CLUSTERS), jnp.int32),
            pltpu.VMEM((STREAMS, BLOCKS, BLOCKS), jnp.int32),
            pltpu.VMEM((STREAMS, ROWS, ROWS), BF16),
            pltpu.VMEM((STREAMS, ROWS, ROWS), BF16),
            pltpu.VMEM((STREAMS, ROWS, ROWS), BF16),
            pltpu.VMEM((STREAMS, ROWS, ROWS), BF16),
            pltpu.VMEM((8, ROWS), F32),
            pltpu.VMEM((GROUP, 8, ROWS), F32),
            pltpu.VMEM((2, Z, STREAMS, ROWS), jnp.int32),
            pltpu.VMEM((2 * Z, ROWS, ROWS), BF16),
            pltpu.VMEM((2 * Z, ROWS, ROWS), BF16),
            pltpu.VMEM((Z, ROWS, ROWS), BF16),
            pltpu.VMEM((Z, ROWS, ROWS), BF16),
            pltpu.VMEM((2 * Z, ROWS, ROWS), BF16),
            pltpu.VMEM((ROWS, ROWS), BF16),
            pltpu.VMEM((Z, ROWS, 2 * ROWS), BF16),
            pltpu.VMEM((Z, ROWS, 1), F32),
            pltpu.VMEM((Z, ROWS, 1), F32),
            pltpu.VMEM((Z, ROWS, ROWS), F32),
            pltpu.VMEM((2 * ROWS, Z * ROWS), F32),
            pltpu.VMEM((2 * ROWS, Z * ROWS), F32),
            pltpu.VMEM((ROWS, 2 * Z * ROWS), BF16),
            pltpu.VMEM((CLUSTERS, 2 * Z * ROWS), BF16),
            sems((6,)),
            sems((3,)),
            sems((1,)),
            sems((1,)),
            sems((1,)),
            sems((1,)),
            sems((1,)),
            sems((2, Z)),
            sems((4,)),
            sems((1,)),
            sems((1,)),
            sems((1,)),
            sems((1,)),
            sems((1,)),
            sems((1,)),
        ],
        compiler_params=pltpu.CompilerParams(collective_id=0, has_side_effects=True),
        name="attend",
    )(query, key, value, q_gain, k_gain, order, cluster_rows, block_map)


def solution(mesh):
    return jax.shard_map(
        local,
        mesh=mesh,
        in_specs=(
            P("head", "seq", None),
            P("head", "seq", None),
            P("head", "seq", None),
            P(),
            P(),
            P("head", "seq"),
            P("head", None),
            P("head", None, None),
        ),
        out_specs=P("head", "seq", None),
        check_vma=False,
    )
```
